256 devices in a mesh: band: 16 (over y_hi, z), slab: 16 (over y_lo, x, core).
Axes of the slice: x: 4, y: 4 (y_hi: 2, y_lo: 2; y = y_hi * 2 + y_lo), z: 8, core: 2. Of those that a mesh axis runs over, the one named last changes fastest.
Arguments:
- orbitals: bfloat16 [64, 160, 160, 160], P('band', 'slab'), may hold values from -4 to 4
- owner: int32 [2], replicated, may hold values from 0 to 15, as said below
- index: int32 [2], replicated, may hold values from 0 to 3, as said below
Outputs:
- exchange: bfloat16 [64, 160, 160, 160], P('band', 'slab')
The draws below stay inside these ranges and needn't reach their ends.
Inputs may be any that keep to these rules, and one draw needn't show every extreme that they name: `owner`: the two partners lie in different band groups, one of them in the last group. `index`: the two positions differ, one of them is the last position of a block.
All inputs are finite; a program needn't handle non-finite values.
Results may differ from the reference program's by a relative error of at most 0.0022.
Values may be sent and summed in bfloat16 or wider, within the bound.
A program may use at most 128 MiB of HBM per device.

```python
import math
import jax
import jax.numpy as jnp
from jax import lax

NX = 160
NY = 160
NZ = 160
BLK = 4
NORB = 64
N_BAND = 16


def draw_orbitals(key, part):
    shape = (NORB, NZ, NX, NY)
    return jax.random.truncated_normal(key, -4.0, 4.0, shape, jnp.float32).astype(jnp.bfloat16)


def pair_with_top(key, count):
    other = jax.random.randint(jax.random.fold_in(key, 1), (), 0, count - 1, dtype=jnp.int32)
    flip = jax.random.randint(jax.random.fold_in(key, 2), (), 0, 2, dtype=jnp.int32)
    top = jnp.int32(count - 1)
    first = jnp.where(flip == 1, other, top)
    second = jnp.where(flip == 1, top, other)
    return jnp.stack([first, second]).astype(jnp.int32)


def draw_owner(key, part):
    return pair_with_top(jax.random.fold_in(key, 101), N_BAND)


def draw_index(key, part):
    return pair_with_top(jax.random.fold_in(key, 202), BLK)


def setup_inputs(seed: int = 0) -> dict:
    key_of = jax.random.split(jax.random.key(seed), 4)
    return {
        "orbitals": draw_orbitals(jax.random.fold_in(key_of[3], 71), 0),
        "owner": draw_owner(jax.random.fold_in(key_of[3], 71), 0),
        "index": draw_index(jax.random.fold_in(key_of[3], 71), 0),
    }


spacing = 0.293125


def hartley(grid):
    for axis in range(3):
        spectrum = jnp.fft.fft(grid, axis=axis)
        grid = (spectrum.real - spectrum.imag).astype(grid.dtype)
    return grid


def squared_wave(count):
    steps = jnp.arange(count, dtype=jnp.int32)
    folded = jnp.where(steps <= count // 2, steps, steps - count).astype(jnp.float32)
    wave = 2.0 * math.pi * folded / (count * spacing)
    return wave * wave


def coulomb():
    g_sq = squared_wave(NZ)[:, None, None] + squared_wave(NX)[None, :, None] + squared_wave(NY)[None, None, :]
    safe = jnp.where(g_sq > 0, g_sq, jnp.float32(1.0))
    return jnp.where(g_sq > 0, 4.0 * math.pi / safe, jnp.float32(0.0)) / (NX * NY * NZ)


def reference(orbitals, owner, index):
    kernel = coulomb()
    total = jnp.zeros((NORB, NZ, NX, NY), jnp.float32)
    for which in range(2):
        row = (owner[which] * BLK + index[which]).astype(jnp.int32)
        partner = lax.dynamic_index_in_dim(orbitals, row, 0, keepdims=False).astype(jnp.float32)

        def one_band(band):
            density = band.astype(jnp.float32) * partner
            potential = hartley(kernel * hartley(density))
            return partner * potential

        total = total + lax.map(one_band, orbitals)
    return (-0.25 * total).astype(jnp.bfloat16)
```

```python
import math

import jax
import jax.numpy as jnp
from jax import lax
from jax.experimental import pallas as pl
from jax.experimental.pallas import tpu as pltpu
from jax.sharding import PartitionSpec as P

spacing = 0.293125
exact = lax.Precision.HIGHEST
MESH = pl.DeviceIdType.MESH
CH = 125


def share_kernel(x_ref, out_ref, recv, sem):
    n = lax.axis_size("band")
    me = lax.axis_index("band")
    last = n - 1
    barrier = pltpu.get_barrier_semaphore()

    @pl.loop(1, n)
    def _(k):
        pl.semaphore_signal(
            barrier, inc=1, device_id={"band": lax.rem(me + k, n)}, device_id_type=MESH
        )

    pl.semaphore_wait(barrier, n - 1)

    def to(src, dst, k, which):
        return pltpu.make_async_remote_copy(
            src_ref=src,
            dst_ref=dst,
            send_sem=sem.at[2 * which],
            recv_sem=sem.at[2 * which + 1],
            device_id={"band": lax.rem(me + k, n)},
            device_id_type=MESH,
        )

    @pl.when(me == last)
    def _():
        @pl.loop(1, n)
        def _(k):
            c = lax.rem(me + k, n)
            to(x_ref.at[0, c], out_ref.at[0, c], k, 0).start()

    @pl.loop(1, n)
    def _(k):
        c = lax.rem(me + k, n)
        to(x_ref.at[1, c], recv.at[me], k, 1).start()

    @pl.when(me == last)
    def _():
        out_ref[0, last] = x_ref[0, last]

    @pl.when(me != last)
    def _():
        to(out_ref.at[0, me], out_ref.at[0, me], 1, 0).wait_recv()

    @pl.loop(1, n)
    def _(k):
        to(out_ref.at[0, me], out_ref.at[0, me], k, 2).start()

    rest = pl.ds(0, n - 1)
    recv[me] = x_ref[1, me]
    to(recv.at[rest], recv.at[rest], 1, 1).wait_recv()
    total = recv[0].astype(jnp.float32)
    for s in range(1, n):
        total = total + recv[s].astype(jnp.float32)
    out_ref[1, me] = total.astype(jnp.bfloat16)

    @pl.loop(1, n)
    def _(k):
        to(out_ref.at[1, me], out_ref.at[1, me], k, 3).start()

    for which in (2, 3):
        to(recv.at[rest], recv.at[rest], 1, which).wait_recv()
        to(recv.at[rest], recv.at[rest], 1, which).wait_send()
    to(recv.at[rest], recv.at[rest], 1, 1).wait_send()

    @pl.when(me == last)
    def _():
        to(recv.at[rest], recv.at[rest], 1, 0).wait_send()


def partners(orbitals, owner, index):
    n = lax.axis_size("band")
    lead = jnp.where(owner[0] == n - 1, 0, 1)
    other = 1 - lead
    a = lax.dynamic_index_in_dim(orbitals, index[lead], 0, keepdims=False)
    b = lax.dynamic_index_in_dim(orbitals, index[other], 0, keepdims=False)
    b = jnp.where(lax.axis_index("band") == owner[other], b, jnp.zeros_like(b))
    shape = a.shape
    chunks = jnp.stack([a, b]).reshape(2, n, CH, 128)
    out = pl.pallas_call(
        share_kernel,
        out_shape=jax.ShapeDtypeStruct(chunks.shape, jnp.bfloat16),
        in_specs=[pl.BlockSpec(memory_space=pltpu.VMEM)],
        out_specs=pl.BlockSpec(memory_space=pltpu.VMEM),
        scratch_shapes=[
            pltpu.VMEM((n, CH, 128), jnp.bfloat16),
            pltpu.SemaphoreType.DMA((8,)),
        ],
        compiler_params=pltpu.CompilerParams(collective_id=0, has_side_effects=True),
        name="share_partners",
    )(chunks)
    return out.reshape((2,) + shape)


def cas_table(count):
    steps = jnp.arange(count, dtype=jnp.int32)
    product = steps[:, None] * steps[None, :] % count
    angle = 2.0 * math.pi / count * product.astype(jnp.float32)
    return jnp.cos(angle) + jnp.sin(angle)


def squared_wave(steps, count):
    folded = jnp.where(steps <= count // 2, steps, steps - count).astype(jnp.float32)
    wave = 2.0 * math.pi * folded / (count * spacing)
    return wave * wave


def coulomb_slice(depth, first, width, across):
    along_z = squared_wave(jnp.arange(depth, dtype=jnp.int32), depth)
    along_x = squared_wave(
        first + jnp.arange(width, dtype=jnp.int32), width * lax.axis_size("slab")
    )
    along_y = squared_wave(jnp.arange(across, dtype=jnp.int32), across)
    g_sq = along_z[:, None, None] + along_x[None, :, None] + along_y[None, None, :]
    safe = jnp.where(g_sq > 0, g_sq, jnp.float32(1.0))
    whole = depth * width * lax.axis_size("slab") * across
    return jnp.where(g_sq > 0, 4.0 * math.pi / safe, jnp.float32(0.0)) / whole


def along_x(grid, table):
    return jnp.einsum(
        "pzxy,xk->pzky", grid, table, precision=exact, preferred_element_type=jnp.float32
    )


def along_y(grid, table):
    return jnp.einsum(
        "pzxy,yk->pzxk", grid, table, precision=exact, preferred_element_type=jnp.float32
    )


def along_z(grid, table):
    return jnp.einsum(
        "pzxy,zk->pkxy", grid, table, precision=exact, preferred_element_type=jnp.float32
    )


def solve(density, tables, kernel):
    table_x, table_y, table_z = tables
    spectrum = along_x(density, table_x)
    spectrum = along_y(spectrum, table_y)
    scaled = (
        along_z(lax.all_to_all(spectrum, "slab", split_axis=2, concat_axis=1, tiled=True), table_z)
        * kernel[None]
    )
    back = along_z(scaled, table_z)
    potential = lax.all_to_all(back, "slab", split_axis=1, concat_axis=2, tiled=True)
    potential = along_y(potential, table_y)
    return along_x(potential, table_x)


def per_device(orbitals, owner, index):
    block, depth_local, width, across = orbitals.shape
    slabs = lax.axis_size("slab")
    depth = depth_local * slabs
    width_local = width // slabs
    tables = (cas_table(width), cas_table(across), cas_table(depth))
    first = lax.axis_index("slab") * width_local
    kernel = coulomb_slice(depth, first, width_local, across)
    bands = orbitals.astype(jnp.float32)
    total = jnp.zeros(orbitals.shape, jnp.float32)
    both = partners(orbitals, owner, index).astype(jnp.float32)
    for which in range(2):
        partner = both[which]
        potential = solve(bands * partner[None], tables, kernel)
        total = total + partner[None] * potential
    return (-0.25 * total).astype(jnp.bfloat16)


def solution(mesh):
    placed = (P("band", "slab", None, None), P(), P())
    return jax.shard_map(
        per_device,
        mesh=mesh,
        in_specs=placed,
        out_specs=P("band", "slab", None, None),
        check_vma=False,
    )
```

```python
import math

import jax
import jax.numpy as jnp
import ml_dtypes
import numpy as np
from jax import lax
from jax.experimental import pallas as pl
from jax.experimental.pallas import tpu as pltpu
from jax.sharding import PartitionSpec as P

spacing = 0.293125
MESH = pl.DeviceIdType.MESH
CH = 125
BF = jnp.bfloat16
F32 = jnp.float32
N = 160
S = 16
L = N // S
B = 4
LOW = 32
TILES = 8


def split_table(table):
    high = table.astype(ml_dtypes.bfloat16)
    low = (table - high.astype(np.float64)).astype(ml_dtypes.bfloat16)
    return high, low


def make_tables():
    steps = np.arange(N)
    angle = 2.0 * np.pi / N * (steps[:, None] * steps[None, :] % N)
    cas = np.cos(angle) + np.sin(angle)
    by_size = np.array([(c + 1) // 2 if c % 2 else (N - c // 2) % N for c in range(N)])
    along_y = cas[by_size]
    ty = np.zeros((B, N, 256))
    for q in range(B):
        ty[q, :, :128] = along_y[LOW:].T
        ty[q, :, 128 + LOW * q : 128 + LOW * (q + 1)] = along_y[:LOW].T
    rows = np.array([by_size[(r % L) * S + r // L] for r in range(N)])
    tx = cas[rows]
    tz = np.zeros((B, N, 2, S, 8))
    for i in range(B):
        for h in range(2):
            for e in range(8):
                z = 8 * (i + h) + e - L * i
                if 0 <= z < L:
                    for s in range(S):
                        tz[i, :, h, s, e] = cas[:, s * L + z]
    tr = np.zeros((N, 3, S, 8))
    for h in range(3):
        for e in range(8):
            row = 8 * h + e
            if row < 2 * L:
                for s in range(S):
                    tr[:, h, s, e] = cas[:, s * L + row % L]
    tz = tz.reshape(B, N, 256)
    tr = tr.reshape(N, 384)
    stack = lambda t, axis: np.concatenate(split_table(t), axis=axis)
    pair = lambda t: np.stack(split_table(t))
    return (
        pair(ty),
        stack(tx, 0),
        stack(tz, 1),
        stack(tr, 0),
        pair(np.swapaxes(tz, 1, 2)),
        pair(tr.T),
        stack(tx.T, 0),
        pair(np.swapaxes(ty, 1, 2)),
    )


def dot(a, b):
    return jnp.dot(a, b, preferred_element_type=F32)


def halves(value):
    high = value.astype(BF)
    return high, (value - high.astype(F32)).astype(BF)


def fold(both):
    return both[:N] + both[N:]


def left(table, value):
    high, low = halves(value)
    return fold(dot(table, high)) + dot(table[:N], low)


def solve_kernel(
    phi, par, tyf, txf, tzf, trf, tzi, tri, txi, tyi, out,
    send, recv, back, home, stage, rest, total, kern, send_sem, recv_sem,
):
    me = lax.axis_index("slab")
    barrier = pltpu.get_barrier_semaphore()

    @pl.loop(1, S)
    def _(k):
        pl.semaphore_signal(
            barrier, inc=1, device_id={"slab": lax.rem(me + k, S)}, device_id_type=MESH
        )

    pl.semaphore_wait(barrier, S - 1)

    def remote(src, dst, which, d):
        return pltpu.make_async_remote_copy(
            src_ref=src,
            dst_ref=dst,
            send_sem=send_sem.at[which],
            recv_sem=recv_sem.at[which],
            device_id={"slab": d},
            device_id_type=MESH,
        )

    def coulomb():
        scale = (2.0 * math.pi / (N * spacing)) ** 2
        size = 4.0 * math.pi / (scale * N**3)
        z = lax.broadcasted_iota(jnp.int32, (N, 256), 0)
        lane = lax.broadcasted_iota(jnp.int32, (N, 256), 1)
        z = jnp.minimum(z, N - z)
        second = lane >> 7
        lane = lane & 127

        @pl.loop(0, L // 2)
        def _(kp):
            x = ((2 * kp + second) * S + me + 1) >> 1
            for u, y in enumerate(((lane + LOW + 1) >> 1, ((lane & (LOW - 1)) + 1) >> 1)):
                g = (z * z + x * x + y * y).astype(F32)
                kern[u, kp] = jnp.where(g > 0, size / jnp.where(g > 0, g, 1.0), 0.0)

    def place(row):
        return lax.div(row, 8), pl.ds(lax.rem(row, 8), N, stride=8)

    def flush(j, t):
        @pl.loop(0, S)
        def _(d):
            block = stage[t, pl.ds(d * 8 * L, 8 * L)].reshape(L, 8, 128)
            send[j, t, pl.ds(d * L, L)] = block.astype(BF)

        recv[j, t, me] = send[j, t, pl.ds(me * L, L)]

        @pl.loop(1, S)
        def _(k):
            d = lax.rem(me + k, S)
            remote(send.at[j, t, pl.ds(d * L, L)], recv.at[j, t, me], j, d).start()

    def forward(j):
        stage[TILES - 1] = jnp.zeros((8 * N, 128), F32)
        rest[...] = jnp.zeros((L, N, 128), F32)

        @pl.loop(0, B)
        def _(i):
            @pl.loop(0, L // 2)
            def _(zz):
                two = pl.ds(2 * zz, 2)
                density = phi[i, two].astype(F32) * par[j, two].astype(F32)
                high, low = halves(density.reshape(2 * N, N))
                y = dot(high, tyf[0, i]) + dot(low, tyf[0, i]) + dot(high, tyf[1, i])
                rest[two] += y[:, 128:].reshape(2, N, 128)
                main = jnp.concatenate([y[:N, :128], y[N:, :128]], axis=1)
                x = left(txf[...], main)
                for b in range(2):
                    t, at = place(i * L + 2 * zz + b)
                    stage[t, at, :] = x[:, 128 * b : 128 * (b + 1)]

            flush(j, i)

        flush(j, B)

        @pl.loop(0, L // 2)
        def _(zz):
            low = jnp.concatenate([rest[2 * zz], rest[2 * zz + 1]], axis=1)
            x = left(txf[...], low)
            left_over = x - x.astype(BF).astype(F32)
            for b in range(2):
                t, at = place(B * L + 2 * zz + b)
                stage[t, at, :] = x[:, 128 * b : 128 * (b + 1)]
                t, at = place((B + 1) * L + 2 * zz + b)
                stage[t, at, :] = left_over[:, 128 * b : 128 * (b + 1)]

        for t in range(B + 1, TILES):
            flush(j, t)

    def middle(j):
        others = recv.at[j, :, pl.ds(0, S - 1)]
        remote(others, others, j, 0).wait_recv()

        @pl.loop(0, L // 2)
        def _(kp):
            def arrived(tiles):
                return jnp.concatenate(
                    [
                        jnp.concatenate(
                            [
                                recv[j, t, :, 2 * kp + b].astype(F32).reshape(128, 128)
                                for t in tiles
                            ],
                            axis=0,
                        )
                        for b in range(2)
                    ],
                    axis=1,
                ).astype(BF)

            def leave(t, value):
                for b in range(2):
                    part = value[:, 128 * b : 128 * (b + 1)].reshape(S, 8, 128)
                    back[j, :, 2 * kp + b, t] = part.astype(BF)

            carry = None
            for i in range(B):
                spectrum = fold(dot(tzf[i], arrived((i, i + 1)))) * kern[0, kp]
                high, low = halves(spectrum)
                w = dot(tzi[0, i], high) + dot(tzi[1, i], high) + dot(tzi[0, i], low)
                leave(i, w[:128] if carry is None else carry + w[:128])
                carry = w[128:]
            leave(B, carry)
            spectrum = fold(dot(trf[...], arrived((5, 6, 7)))) * kern[1, kp]
            high, low = halves(spectrum)
            w = dot(tri[0], high) + dot(tri[1], high) + dot(tri[0], low)
            left_over = w - w.astype(BF).astype(F32)
            e = lax.broadcasted_iota(jnp.int32, (128, 256), 0) & 7
            leave(5, w[:128])
            leave(6, jnp.where(e < 2, w[128:256], left_over[128:256]))
            leave(7, left_over[256:])

            home[j, pl.ds(me * L + 2 * kp, 2)] = back[j, me, pl.ds(2 * kp, 2)]

            @pl.loop(1, S)
            def _(k):
                d = lax.rem(me + k, S)
                remote(
                    back.at[j, d, pl.ds(2 * kp, 2)],
                    home.at[j, pl.ds(me * L + 2 * kp, 2)],
                    2 + j,
                    d,
                ).start()

    def inverse(j):
        others = home.at[j, pl.ds(0, N - L)]
        remote(others, others, 2 + j, 0).wait_recv()

        for t in range(TILES):
            @pl.loop(0, S)
            def _(c):
                block = home[j, pl.ds(c * L, L), t].astype(F32)
                stage[t, pl.ds(c * 8 * L, 8 * L)] = block.reshape(8 * L, 128)

        @pl.loop(0, L // 2)
        def _(zz):
            def planes(row):
                got = []
                for b in range(2):
                    t, at = place(row + 2 * zz + b)
                    got.append(stage[t, at, :])
                return jnp.concatenate(got, axis=1).astype(BF)

            low_y = fold(dot(txi[...], planes(B * L))) + dot(txi[:N], planes((B + 1) * L))
            two = pl.ds(2 * zz, 2)
            partner = par[j, two].astype(F32)
            for i in range(B):
                main = fold(dot(txi[...], planes(i * L)))
                u = jnp.concatenate(
                    [
                        jnp.concatenate([main[:, :128], low_y[:, :128]], axis=1),
                        jnp.concatenate([main[:, 128:], low_y[:, 128:]], axis=1),
                    ],
                    axis=0,
                )
                high, low = halves(u)
                v = dot(high, tyi[0, i]) + dot(low, tyi[0, i]) + dot(high, tyi[1, i])
                v = v.reshape(2, N, N) * partner
                if j == 0:
                    total[i, two] = v
                else:
                    out[i, two] = (-0.25 * (total[i, two] + v)).astype(BF)

    coulomb()
    pl.loop(0, 2)(forward)
    pl.loop(0, 2)(middle)
    for j in range(2):
        inverse(j)
    for j in range(2):
        sent = send.at[j, :, pl.ds(0, N - L)]
        remote(sent, sent, j, 0).wait_send()
        sent = back.at[j, pl.ds(0, S - 1)]
        remote(sent, sent, 2 + j, 0).wait_send()


def solve(orbitals, both):
    tables = [jnp.asarray(t) for t in make_tables()]
    vmem = pl.BlockSpec(memory_space=pltpu.VMEM)
    return pl.pallas_call(
        solve_kernel,
        out_shape=jax.ShapeDtypeStruct(orbitals.shape, BF),
        in_specs=[vmem] * (2 + len(tables)),
        out_specs=vmem,
        scratch_shapes=[
            pltpu.VMEM((2, TILES, N, 8, 128), BF),
            pltpu.VMEM((2, TILES, S, L, 8, 128), BF),
            pltpu.VMEM((2, S, L, TILES, 8, 128), BF),
            pltpu.VMEM((2, N, TILES, 8, 128), BF),
            pltpu.VMEM((TILES, 8 * N, 128), F32),
            pltpu.VMEM((L, N, 128), F32),
            pltpu.VMEM((B, L, N, N), F32),
            pltpu.VMEM((2, L // 2, N, 256), F32),
            pltpu.SemaphoreType.DMA((4,)),
            pltpu.SemaphoreType.DMA((4,)),
        ],
        compiler_params=pltpu.CompilerParams(
            collective_id=1, has_side_effects=True, vmem_limit_bytes=60 << 20
        ),
        name="solve_pairs",
    )(orbitals, both, *tables)


def share_kernel(x_ref, out_ref, recv, sem):
    n = lax.axis_size("band")
    me = lax.axis_index("band")
    last = n - 1
    barrier = pltpu.get_barrier_semaphore()

    @pl.loop(1, n)
    def _(k):
        pl.semaphore_signal(
            barrier, inc=1, device_id={"band": lax.rem(me + k, n)}, device_id_type=MESH
        )

    pl.semaphore_wait(barrier, n - 1)

    def to(src, dst, k, which):
        return pltpu.make_async_remote_copy(
            src_ref=src,
            dst_ref=dst,
            send_sem=sem.at[2 * which],
            recv_sem=sem.at[2 * which + 1],
            device_id={"band": lax.rem(me + k, n)},
            device_id_type=MESH,
        )

    @pl.when(me == last)
    def _():
        @pl.loop(1, n)
        def _(k):
            c = lax.rem(me + k, n)
            to(x_ref.at[0, c], out_ref.at[0, c], k, 0).start()

    @pl.loop(1, n)
    def _(k):
        c = lax.rem(me + k, n)
        to(x_ref.at[1, c], recv.at[me], k, 1).start()

    @pl.when(me == last)
    def _():
        out_ref[0, last] = x_ref[0, last]

    @pl.when(me != last)
    def _():
        to(out_ref.at[0, me], out_ref.at[0, me], 1, 0).wait_recv()

    @pl.loop(1, n)
    def _(k):
        to(out_ref.at[0, me], out_ref.at[0, me], k, 2).start()

    rest = pl.ds(0, n - 1)
    recv[me] = x_ref[1, me]
    to(recv.at[rest], recv.at[rest], 1, 1).wait_recv()
    total = recv[0].astype(jnp.float32)
    for s in range(1, n):
        total = total + recv[s].astype(jnp.float32)
    out_ref[1, me] = total.astype(jnp.bfloat16)

    @pl.loop(1, n)
    def _(k):
        to(out_ref.at[1, me], out_ref.at[1, me], k, 3).start()

    for which in (2, 3):
        to(recv.at[rest], recv.at[rest], 1, which).wait_recv()
        to(recv.at[rest], recv.at[rest], 1, which).wait_send()
    to(recv.at[rest], recv.at[rest], 1, 1).wait_send()

    @pl.when(me == last)
    def _():
        to(recv.at[rest], recv.at[rest], 1, 0).wait_send()


def partners(orbitals, owner, index):
    n = lax.axis_size("band")
    lead = jnp.where(owner[0] == n - 1, 0, 1)
    other = 1 - lead
    a = lax.dynamic_index_in_dim(orbitals, index[lead], 0, keepdims=False)
    b = lax.dynamic_index_in_dim(orbitals, index[other], 0, keepdims=False)
    b = jnp.where(lax.axis_index("band") == owner[other], b, jnp.zeros_like(b))
    shape = a.shape
    chunks = jnp.stack([a, b]).reshape(2, n, CH, 128)
    out = pl.pallas_call(
        share_kernel,
        out_shape=jax.ShapeDtypeStruct(chunks.shape, jnp.bfloat16),
        in_specs=[pl.BlockSpec(memory_space=pltpu.VMEM)],
        out_specs=pl.BlockSpec(memory_space=pltpu.VMEM),
        scratch_shapes=[
            pltpu.VMEM((n, CH, 128), jnp.bfloat16),
            pltpu.SemaphoreType.DMA((8,)),
        ],
        compiler_params=pltpu.CompilerParams(collective_id=0, has_side_effects=True),
        name="share_partners",
    )(chunks)
    return out.reshape((2,) + shape)


def per_device(orbitals, owner, index):
    return solve(orbitals, partners(orbitals, owner, index))


def solution(mesh):
    placed = (P("band", "slab", None, None), P(), P())
    return jax.shard_map(
        per_device,
        mesh=mesh,
        in_specs=placed,
        out_specs=P("band", "slab", None, None),
        check_vma=False,
    )
```

```python
import math

import jax
import jax.numpy as jnp
import ml_dtypes
import numpy as np
from jax import lax
from jax.experimental import pallas as pl
from jax.experimental.pallas import tpu as pltpu
from jax.sharding import PartitionSpec as P

spacing = 0.293125
MESH = pl.DeviceIdType.MESH
CH = 128
BF = jnp.bfloat16
F32 = jnp.float32
N = 160
S = 16
L = N // S
B = 4
LOW = 32
TILES = 8


def split_table(table):
    high = table.astype(ml_dtypes.bfloat16)
    low = (table - high.astype(np.float64)).astype(ml_dtypes.bfloat16)
    return high, low


def make_tables():
    steps = np.arange(N)
    angle = 2.0 * np.pi / N * (steps[:, None] * steps[None, :] % N)
    cas = np.cos(angle) + np.sin(angle)
    by_size = np.array([(c + 1) // 2 if c % 2 else (N - c // 2) % N for c in range(N)])
    along_y = cas[by_size]
    ty = np.zeros((B, N, 256))
    for q in range(B):
        ty[q, :, :128] = along_y[LOW:].T
        ty[q, :, 128 + LOW * q : 128 + LOW * (q + 1)] = along_y[:LOW].T
    rows = np.array([by_size[(r % L) * S + r // L] for r in range(N)])
    tx = cas[rows]
    tz = np.zeros((B, N, 2, S, 8))
    for i in range(B):
        for h in range(2):
            for e in range(8):
                z = 8 * (i + h) + e - L * i
                if 0 <= z < L:
                    for s in range(S):
                        tz[i, :, h, s, e] = cas[:, s * L + z]
    tr = np.zeros((N, 3, S, 8))
    for h in range(3):
        for e in range(8):
            row = 8 * h + e
            if row < 2 * L:
                for s in range(S):
                    tr[:, h, s, e] = cas[:, s * L + row % L]
    tz = tz.reshape(B, N, 256)
    tr = tr.reshape(N, 384)
    stack = lambda t, axis: np.concatenate(split_table(t), axis=axis)
    pair = lambda t: np.stack(split_table(t))
    return (
        pair(ty),
        stack(tx, 0),
        stack(tz, 1),
        stack(tr, 0),
        pair(np.swapaxes(tz, 1, 2)),
        pair(tr.T),
        stack(tx.T, 0),
        pair(np.swapaxes(ty, 1, 2)),
    )


def dot(a, b):
    return jnp.dot(a, b, preferred_element_type=F32)


def halves(value):
    high = value.astype(BF)
    return high, (value - high.astype(F32)).astype(BF)


def fold(both):
    return both[:N] + both[N:]


def left(table, value):
    high, low = halves(value)
    return fold(dot(table, high)) + dot(table[:N], low)


def solve_kernel(
    owner, index, phi, tyf, txf, tzf, trf, tzi, tri, txi, tyi, out,
    chosen, masked, heap, gathered, par, send, recv, back, home, stage, rest, rest_parts,
    carry, total, kern, send_sem, recv_sem, share_send, share_recv,
):
    me = lax.axis_index("slab")
    band = lax.axis_index("band")
    bands = lax.axis_size("band")
    last = bands - 1
    barrier = pltpu.get_barrier_semaphore()

    @pl.loop(1, S)
    def _(k):
        pl.semaphore_signal(
            barrier, inc=1, device_id={"slab": lax.rem(me + k, S)}, device_id_type=MESH
        )

    @pl.loop(1, bands)
    def _(k):
        pl.semaphore_signal(
            barrier, inc=1, device_id={"band": lax.rem(band + k, bands)}, device_id_type=MESH
        )

    pl.semaphore_wait(barrier, S + bands - 2)

    def remote(src, dst, which, t, d):
        return pltpu.make_async_remote_copy(
            src_ref=src,
            dst_ref=dst,
            send_sem=send_sem.at[which, t],
            recv_sem=recv_sem.at[which, t],
            device_id={"slab": d},
            device_id_type=MESH,
        )

    def share(src, dst, which, d):
        return pltpu.make_async_remote_copy(
            src_ref=src,
            dst_ref=dst,
            send_sem=share_send.at[which],
            recv_sem=share_recv.at[which],
            device_id={"band": d},
            device_id_type=MESH,
        )

    def chunk(c):
        return pl.ds(pl.multiple_of(c * CH, CH), CH)

    def pick(flat, weights):
        flat[pl.ds(N * L * 5 // 4, 48)] = jnp.zeros((48, 128), BF)

        @pl.loop(0, L // 2)
        def _(zz):
            two = pl.ds(2 * zz, 2)
            plane = phi[0, two].astype(F32) * weights[0]
            for i in range(1, B):
                plane = plane + phi[i, two].astype(F32) * weights[i]
            flat[pl.ds(pl.multiple_of(2 * N * zz, 2 * N), 2 * N)] = (
                plane[:, :, :128].reshape(2 * N, 128).astype(BF)
            )
            tail = [
                jnp.concatenate([plane[b, 40 * q : 40 * q + 40, 128:] for q in range(4)], axis=1)
                for b in range(2)
            ]
            flat[pl.ds(pl.multiple_of(N * L + 80 * zz, 80), 80)] = (
                jnp.concatenate(tail, axis=0).astype(BF)
            )

    def unpack(j):
        @pl.loop(0, L // 2)
        def _(zz):
            main = gathered[j, pl.ds(pl.multiple_of(2 * N * zz, 2 * N), 2 * N)].astype(F32)
            par[j, pl.ds(2 * zz, 2), :, :128] = main.reshape(2, N, 128)
            tail = gathered[j, pl.ds(pl.multiple_of(N * L + 80 * zz, 80), 80)].astype(F32)
            for b in range(2):
                for q in range(4):
                    par[j, 2 * zz + b, 40 * q : 40 * q + 40, 128:] = tail[
                        40 * b : 40 * b + 40, 32 * q : 32 * q + 32
                    ]

    def coulomb():
        scale = (2.0 * math.pi / (N * spacing)) ** 2
        size = 4.0 * math.pi / (scale * N**3)
        z = lax.broadcasted_iota(jnp.int32, (N, 256), 0)
        lane = lax.broadcasted_iota(jnp.int32, (N, 256), 1)
        z = jnp.minimum(z, N - z)
        second = lane >> 7
        lane = lane & 127

        @pl.loop(0, L // 2)
        def _(kp):
            x = ((2 * kp + second) * S + me + 1) >> 1
            for u, y in enumerate(((lane + LOW + 1) >> 1, ((lane & (LOW - 1)) + 1) >> 1)):
                g = (z * z + x * x + y * y).astype(F32)
                kern[u, kp] = jnp.where(g > 0, size / jnp.where(g > 0, g, 1.0), 0.0)

    def place(row):
        return lax.div(row, 8), pl.ds(lax.rem(row, 8), N, stride=8)

    def modes(t):
        return 2 if isinstance(t, int) and t == TILES - 1 else L

    def flush(j, t):
        m = modes(t)

        @pl.loop(0, S)
        def _(d):
            block = stage[t, pl.ds(d * 8 * L, 8 * m)].reshape(m, 8, 128)
            send[j, t, pl.ds(d * L, m)] = block.astype(BF)

        recv[j, t, me, pl.ds(0, m)] = send[j, t, pl.ds(me * L, m)]

        @pl.loop(1, S)
        def _(k):
            d = lax.rem(me + k, S)
            remote(
                send.at[j, t, pl.ds(d * L, m)], recv.at[j, t, me, pl.ds(0, m)], j, t, d
            ).start()

    def forward(j, between):
        rest[...] = jnp.zeros((L, N, 128), F32)

        @pl.loop(0, B)
        def _(i):
            @pl.loop(0, L // 2)
            def _(zz):
                two = pl.ds(2 * zz, 2)
                density = phi[i, two].astype(F32) * par[j, two]
                high, low = halves(density.reshape(2 * N, N))
                y = dot(high, tyf[0, i]) + dot(low, tyf[0, i]) + dot(high, tyf[1, i])
                rest[two] += y[:, 128:].reshape(2, N, 128)
                main = jnp.concatenate([y[:N, :128], y[N:, :128]], axis=1)
                x = left(txf[...], main)
                for b in range(2):
                    t, at = place(i * L + 2 * zz + b)
                    stage[t, at, :] = x[:, 128 * b : 128 * (b + 1)]

            flush(j, i)
            if between is not None:
                pl.when(i == 0)(between)

        flush(j, B)

        @pl.loop(0, L // 2)
        def _(zz):
            low = jnp.concatenate([rest[2 * zz], rest[2 * zz + 1]], axis=1)
            x = left(txf[...], low)
            left_over = x - x.astype(BF).astype(F32)
            for b in range(2):
                t, at = place(B * L + 2 * zz + b)
                stage[t, at, :] = x[:, 128 * b : 128 * (b + 1)]
                t, at = place((B + 1) * L + 2 * zz + b)
                stage[t, at, :] = left_over[:, 128 * b : 128 * (b + 1)]

        for t in range(B + 1, TILES):
            flush(j, t)

    def arrived(j, t):
        m = modes(t)
        others = recv.at[j, t, pl.ds(0, S - 1), pl.ds(0, m)]
        remote(others, others, j, t, 0).wait_recv()

    def returned(j, t):
        m = modes(t)
        others = back.at[j, t, pl.ds(0, S - 1), pl.ds(0, m)]
        remote(others, others, 2 + j, t, 0).wait_recv()

    def middle(j):
        def load(kp, tiles):
            return jnp.concatenate(
                [
                    jnp.concatenate(
                        [recv[j, t, :, 2 * kp + b].astype(F32).reshape(128, 128) for t in tiles],
                        axis=0,
                    )
                    for b in range(2)
                ],
                axis=1,
            ).astype(BF)

        def leave(kp, t, value):
            for b in range(2):
                part = value[:, 128 * b : 128 * (b + 1)].reshape(S, 8, 128)
                back[j, t, :, 2 * kp + b] = part.astype(BF)

        def ship(t):
            m = modes(t)
            home[j, t, pl.ds(me * L, m)] = back[j, t, me, pl.ds(0, m)]

            @pl.loop(1, S)
            def _(k):
                d = lax.rem(me + k, S)
                remote(
                    back.at[j, t, d, pl.ds(0, m)], home.at[j, t, pl.ds(me * L, m)], 2 + j, t, d
                ).start()

        def low_modes(kp, tiles):
            k = 128 * len(tiles)
            spectrum = fold(dot(trf[:, :k], load(kp, tiles))) * kern[1, kp]
            high, low = halves(spectrum)
            w = dot(tri[0, :k], high) + dot(tri[1, :k], high) + dot(tri[0, :k], low)
            left_over = w - w.astype(BF).astype(F32)
            e = lax.broadcasted_iota(jnp.int32, (128, 256), 0) & 7
            leave(kp, 5, w[:128])
            leave(kp, 6, jnp.where(e < 2, w[128:256], left_over[128:256]))
            if len(tiles) == 3:
                leave(kp, 7, left_over[256:])

        for t in range(B + 1, TILES):
            arrived(j, t)
        low_modes(0, (5, 6, 7))

        @pl.loop(1, L // 2)
        def _(kp):
            low_modes(kp, (5, 6))

        for t in range(B + 1, TILES):
            ship(t)
        arrived(j, 0)
        carry[...] = jnp.zeros((L // 2, 128, 256), F32)

        @pl.loop(0, B)
        def _(i):
            arrived(j, i + 1)

            @pl.loop(0, L // 2)
            def _(kp):
                spectrum = fold(dot(tzf[i], load(kp, (i, i + 1)))) * kern[0, kp]
                high, low = halves(spectrum)
                w = dot(tzi[0, i], high) + dot(tzi[1, i], high) + dot(tzi[0, i], low)
                leave(kp, i, carry[kp] + w[:128])
                carry[kp] = w[128:]

            ship(i)

        @pl.loop(0, L // 2)
        def _(kp):
            leave(kp, B, carry[kp])

        ship(B)

    def inverse(j):
        def unstage(t):
            m = modes(t)

            @pl.loop(0, S)
            def _(c):
                block = home[j, t, pl.ds(c * L, m)].astype(F32)
                stage[t, pl.ds(c * 8 * L, 8 * m)] = block.reshape(8 * m, 128)

        def planes(row):
            got = []
            for b in range(2):
                t, at = place(row + b)
                got.append(stage[t, at, :])
            return jnp.concatenate(got, axis=1).astype(BF)

        stage[TILES - 1] = jnp.zeros((8 * N, 128), F32)
        for t in range(B + 1, TILES):
            returned(j, t)
            unstage(t)

        @pl.loop(0, L // 2)
        def _(zz):
            row = B * L + 2 * zz
            low_y = fold(dot(txi[...], planes(row))) + dot(txi[:N], planes(row + L))
            for h, part in enumerate(halves(low_y)):
                for b in range(2):
                    rest_parts[h, 2 * zz + b] = part[:, 128 * b : 128 * (b + 1)]

        returned(j, 0)
        unstage(0)

        @pl.loop(0, B)
        def _(i):
            returned(j, i + 1)
            unstage(i + 1)

            @pl.loop(0, L // 2)
            def _(zz):
                two = pl.ds(2 * zz, 2)
                main = halves(fold(dot(txi[...], planes(i * L + 2 * zz))))
                high, low = (
                    jnp.concatenate(
                        [
                            jnp.concatenate(
                                [main[h][:, 128 * b : 128 * (b + 1)], rest_parts[h, 2 * zz + b]],
                                axis=1,
                            )
                            for b in range(2)
                        ],
                        axis=0,
                    )
                    for h in range(2)
                )
                v = dot(high, tyi[0, i]) + dot(low, tyi[0, i]) + dot(high, tyi[1, i])
                v = v.reshape(2, N, N) * par[j, two]
                if j == 0:
                    total[i, two] = v
                else:
                    out[i, two] = (-0.25 * (total[i, two] + v)).astype(BF)

    first = owner[0] == last
    index_a = jnp.where(first, index[0], index[1])
    index_b = jnp.where(first, index[1], index[0])
    owner_b = jnp.where(first, owner[1], owner[0])
    others = gathered.at[0, pl.ds(0, (bands - 1) * CH)]

    @pl.when(band == last)
    def _():
        pick(chosen, [jnp.where(index_a == i, 1.0, 0.0) for i in range(B)])

        @pl.loop(1, bands)
        def _(k):
            c = lax.rem(band + k, bands)
            share(chosen.at[chunk(c)], gathered.at[0, chunk(c)], 0, c).start()

        gathered[0, chunk(last)] = chosen[chunk(last)]

    is_b = owner_b == band
    pick(masked, [jnp.where((index_b == i) & is_b, 1.0, 0.0) for i in range(B)])

    @pl.when(band != last)
    def _():
        mine = gathered.at[0, chunk(band)]
        share(mine, mine, 0, 0).wait_recv()

    @pl.loop(1, bands)
    def _(k):
        mine = gathered.at[0, chunk(band)]
        share(mine, mine, 1, lax.rem(band + k, bands)).start()

    @pl.loop(1, bands)
    def _(k):
        c = lax.rem(band + k, bands)
        share(masked.at[chunk(c)], heap.at[band], 2, c).start()

    coulomb()
    share(others, others, 1, 0).wait_recv()
    unpack(0)

    def finish_b():
        share(others, others, 2, 0).wait_recv()
        heap[band] = masked[chunk(band)]
        whole = heap[0].astype(F32)
        for s in range(1, bands):
            whole = whole + heap[s].astype(F32)
        gathered[1, chunk(band)] = whole.astype(BF)

        @pl.loop(1, bands)
        def _(k):
            mine = gathered.at[1, chunk(band)]
            share(mine, mine, 3, lax.rem(band + k, bands)).start()

    stage[TILES - 1] = jnp.zeros((8 * N, 128), F32)
    forward(0, finish_b)
    share(others, others, 3, 0).wait_recv()
    unpack(1)
    forward(1, None)
    for j in range(2):
        middle(j)
    for j in range(2):
        inverse(j)
    for j in range(2):
        for t in range(TILES):
            sent = recv.at[j, t, pl.ds(0, S - 1), pl.ds(0, modes(t))]
            remote(sent, sent, j, t, 0).wait_send()
            remote(sent, sent, 2 + j, t, 0).wait_send()
    for which in range(1, 4):
        share(others, others, which, 0).wait_send()

    @pl.when(band == last)
    def _():
        share(others, others, 0, 0).wait_send()


def solve(orbitals, owner, index):
    tables = [jnp.asarray(t) for t in make_tables()]
    vmem = pl.BlockSpec(memory_space=pltpu.VMEM)
    smem = pl.BlockSpec(memory_space=pltpu.SMEM)
    bands = lax.axis_size("band")
    return pl.pallas_call(
        solve_kernel,
        out_shape=jax.ShapeDtypeStruct(orbitals.shape, BF),
        in_specs=[smem, smem] + [vmem] * (1 + len(tables)),
        out_specs=vmem,
        scratch_shapes=[
            pltpu.VMEM((bands * CH, 128), BF),
            pltpu.VMEM((bands * CH, 128), BF),
            pltpu.VMEM((bands, CH, 128), BF),
            pltpu.VMEM((2, bands * CH, 128), BF),
            pltpu.VMEM((2, L, N, N), F32),
            pltpu.VMEM((2, TILES, N, 8, 128), BF),
            pltpu.VMEM((2, TILES, S, L, 8, 128), BF),
            pltpu.VMEM((2, TILES, S, L, 8, 128), BF),
            pltpu.VMEM((2, TILES, N, 8, 128), BF),
            pltpu.VMEM((TILES, 8 * N, 128), F32),
            pltpu.VMEM((L, N, 128), F32),
            pltpu.VMEM((2, L, N, 128), BF),
            pltpu.VMEM((L // 2, 128, 256), F32),
            pltpu.VMEM((B, L, N, N), F32),
            pltpu.VMEM((2, L // 2, N, 256), F32),
            pltpu.SemaphoreType.DMA((4, TILES)),
            pltpu.SemaphoreType.DMA((4, TILES)),
            pltpu.SemaphoreType.DMA((4,)),
            pltpu.SemaphoreType.DMA((4,)),
        ],
        compiler_params=pltpu.CompilerParams(
            collective_id=0, has_side_effects=True, vmem_limit_bytes=60 << 20
        ),
        name="solve_pairs",
    )(owner, index, orbitals, *tables)


def per_device(orbitals, owner, index):
    return solve(orbitals, owner, index)


def solution(mesh):
    placed = (P("band", "slab", None, None), P(), P())
    return jax.shard_map(
        per_device,
        mesh=mesh,
        in_specs=placed,
        out_specs=P("band", "slab", None, None),
        check_vma=False,
    )
```

```python
import math

import jax
import jax.numpy as jnp
import ml_dtypes
import numpy as np
from jax import lax
from jax.experimental import pallas as pl
from jax.experimental.pallas import tpu as pltpu
from jax.sharding import PartitionSpec as P

spacing = 0.293125
MESH = pl.DeviceIdType.MESH
CH = 128
BF = jnp.bfloat16
F32 = jnp.float32
N = 160
S = 16
L = N // S
B = 4
LOW = 32
TILES = 8


def split_table(table):
    high = table.astype(ml_dtypes.bfloat16)
    low = (table - high.astype(np.float64)).astype(ml_dtypes.bfloat16)
    return high, low


def make_tables():
    steps = np.arange(N)
    angle = 2.0 * np.pi / N * (steps[:, None] * steps[None, :] % N)
    cas = np.cos(angle) + np.sin(angle)
    by_size = np.array([(c + 1) // 2 if c % 2 else (N - c // 2) % N for c in range(N)])
    along_y = cas[by_size]
    ty = np.zeros((B, N, 256))
    for q in range(B):
        ty[q, :, :128] = along_y[LOW:].T
        ty[q, :, 128 + LOW * q : 128 + LOW * (q + 1)] = along_y[:LOW].T
    rows = np.array([by_size[(r % L) * S + r // L] for r in range(N)])
    tx = cas[rows]
    tz = np.zeros((B, N, 2, S, 8))
    for i in range(B):
        for h in range(2):
            for e in range(8):
                z = 8 * (i + h) + e - L * i
                if 0 <= z < L:
                    for s in range(S):
                        tz[i, :, h, s, e] = cas[:, s * L + z]
    tr = np.zeros((N, 3, S, 8))
    for h in range(3):
        for e in range(8):
            row = 8 * h + e
            if row < 2 * L:
                for s in range(S):
                    tr[:, h, s, e] = cas[:, s * L + row % L]
    tz = tz.reshape(B, N, 256)
    tr = tr.reshape(N, 384)
    stack = lambda t, axis: np.concatenate(split_table(t), axis=axis)
    pair = lambda t: np.stack(split_table(t))
    return (
        pair(ty),
        stack(tx, 0),
        stack(tz, 1),
        stack(tr, 0),
        pair(np.swapaxes(tz, 1, 2)),
        pair(tr.T),
        stack(tx.T, 0),
        pair(np.swapaxes(ty, 1, 2)),
    )


def dot(a, b):
    return jnp.dot(a, b, preferred_element_type=F32)


def halves(value):
    high = value.astype(BF)
    return high, (value - high.astype(F32)).astype(BF)


def fold(both):
    return both[:N] + both[N:]


def left(table, value):
    high, low = halves(value)
    return fold(dot(table, high)) + dot(table[:N], low)


def solve_kernel(
    owner, index, orbitals, *refs
):
    tables, out, phi = refs[:8], refs[8], refs[9]
    tyf, txf, tzf, trf, tzi, tri, txi, tyi = held = refs[10:18]
    (
    chosen, masked, heap, part_b, other_b, gathered, par, send, recv, back, home, stage, rest, rest_parts,
    carry, total, kern, load_sem, send_sem, recv_sem, share_send, share_recv,
    ) = refs[18:]
    loads = [
        pltpu.make_async_copy(src, dst, load_sem.at[n])
        for n, (src, dst) in enumerate(zip((orbitals,) + tables, (phi,) + held))
    ]
    for load in loads:
        load.start()
    me = lax.axis_index("slab")
    band = lax.axis_index("band")
    bands = lax.axis_size("band")
    last = bands - 1
    barrier = pltpu.get_barrier_semaphore()

    @pl.loop(1, S)
    def _(k):
        pl.semaphore_signal(
            barrier, inc=1, device_id={"slab": lax.rem(me + k, S)}, device_id_type=MESH
        )

    @pl.loop(1, bands)
    def _(k):
        pl.semaphore_signal(
            barrier, inc=1, device_id={"band": lax.rem(band + k, bands)}, device_id_type=MESH
        )

    def remote(src, dst, which, t, d):
        return pltpu.make_async_remote_copy(
            src_ref=src,
            dst_ref=dst,
            send_sem=send_sem.at[which, t],
            recv_sem=recv_sem.at[which, t],
            device_id={"slab": d},
            device_id_type=MESH,
        )

    def share(src, dst, which, d):
        return pltpu.make_async_remote_copy(
            src_ref=src,
            dst_ref=dst,
            send_sem=share_send.at[which],
            recv_sem=share_recv.at[which],
            device_id={"band": d},
            device_id_type=MESH,
        )

    def chunk(c):
        return pl.ds(pl.multiple_of(c * CH, CH), CH)

    def block(c):
        return pl.ds(pl.multiple_of(c * 2 * CH, 2 * CH), 2 * CH)

    def pick(flat, weights):
        flat[pl.ds(N * L * 5 // 4, 48)] = jnp.zeros((48, 128), BF)

        @pl.loop(0, L // 2)
        def _(zz):
            two = pl.ds(2 * zz, 2)
            plane = phi[0, two].astype(F32) * weights[0]
            for i in range(1, B):
                plane = plane + phi[i, two].astype(F32) * weights[i]
            flat[pl.ds(pl.multiple_of(2 * N * zz, 2 * N), 2 * N)] = (
                plane[:, :, :128].reshape(2 * N, 128).astype(BF)
            )
            tail = [
                jnp.concatenate([plane[b, 40 * q : 40 * q + 40, 128:] for q in range(4)], axis=1)
                for b in range(2)
            ]
            flat[pl.ds(pl.multiple_of(N * L + 80 * zz, 80), 80)] = (
                jnp.concatenate(tail, axis=0).astype(BF)
            )

    def unpack(j):
        @pl.loop(0, L // 2)
        def _(zz):
            main = gathered[j, pl.ds(pl.multiple_of(2 * N * zz, 2 * N), 2 * N)].astype(F32)
            par[j, pl.ds(2 * zz, 2), :, :128] = main.reshape(2, N, 128)
            tail = gathered[j, pl.ds(pl.multiple_of(N * L + 80 * zz, 80), 80)].astype(F32)
            for b in range(2):
                for q in range(4):
                    par[j, 2 * zz + b, 40 * q : 40 * q + 40, 128:] = tail[
                        40 * b : 40 * b + 40, 32 * q : 32 * q + 32
                    ]

    def coulomb():
        scale = (2.0 * math.pi / (N * spacing)) ** 2
        size = 4.0 * math.pi / (scale * N**3)
        z = lax.broadcasted_iota(jnp.int32, (N, 256), 0)
        lane = lax.broadcasted_iota(jnp.int32, (N, 256), 1)
        z = jnp.minimum(z, N - z)
        second = lane >> 7
        lane = lane & 127

        @pl.loop(0, L // 2)
        def _(kp):
            x = ((2 * kp + second) * S + me + 1) >> 1
            for u, y in enumerate(((lane + LOW + 1) >> 1, ((lane & (LOW - 1)) + 1) >> 1)):
                g = (z * z + x * x + y * y).astype(F32)
                kern[u, kp] = jnp.where(g > 0, size / jnp.where(g > 0, g, 1.0), 0.0)

    def place(row):
        return lax.div(row, 8), pl.ds(lax.rem(row, 8), N, stride=8)

    def modes(t):
        return 2 if isinstance(t, int) and t == TILES - 1 else L

    def flush(j, t):
        m = modes(t)

        @pl.loop(0, S)
        def _(d):
            block = stage[t, pl.ds(d * 8 * L, 8 * m)].reshape(m, 8, 128)
            send[j, t, pl.ds(d * L, m)] = block.astype(BF)

        recv[j, t, me, pl.ds(0, m)] = send[j, t, pl.ds(me * L, m)]

        @pl.loop(1, S)
        def _(k):
            d = lax.rem(me + k, S)
            remote(
                send.at[j, t, pl.ds(d * L, m)], recv.at[j, t, me, pl.ds(0, m)], j, t, d
            ).start()

    def forward(j, between):
        rest[...] = jnp.zeros((L, N, 128), F32)

        @pl.loop(0, B)
        def _(i):
            @pl.loop(0, L // 2)
            def _(zz):
                two = pl.ds(2 * zz, 2)
                density = phi[i, two].astype(F32) * par[j, two]
                high, low = halves(density.reshape(2 * N, N))
                y = dot(high, tyf[0, i]) + dot(low, tyf[0, i]) + dot(high, tyf[1, i])
                rest[two] += y[:, 128:].reshape(2, N, 128)
                main = jnp.concatenate([y[:N, :128], y[N:, :128]], axis=1)
                x = left(txf[...], main)
                for b in range(2):
                    t, at = place(i * L + 2 * zz + b)
                    stage[t, at, :] = x[:, 128 * b : 128 * (b + 1)]

            flush(j, i)
            for n, step in enumerate(between):
                pl.when(i == n + 1)(step)

        flush(j, B)

        @pl.loop(0, L // 2)
        def _(zz):
            low = jnp.concatenate([rest[2 * zz], rest[2 * zz + 1]], axis=1)
            x = left(txf[...], low)
            left_over = x - x.astype(BF).astype(F32)
            for b in range(2):
                t, at = place(B * L + 2 * zz + b)
                stage[t, at, :] = x[:, 128 * b : 128 * (b + 1)]
                t, at = place((B + 1) * L + 2 * zz + b)
                stage[t, at, :] = left_over[:, 128 * b : 128 * (b + 1)]

        for t in range(B + 1, TILES):
            flush(j, t)

    def arrived(j, t):
        m = modes(t)
        others = recv.at[j, t, pl.ds(0, S - 1), pl.ds(0, m)]
        remote(others, others, j, t, 0).wait_recv()

    def returned(j, t):
        m = modes(t)
        others = back.at[j, t, pl.ds(0, S - 1), pl.ds(0, m)]
        remote(others, others, 2 + j, t, 0).wait_recv()

    def middle(j):
        def load(kp, tiles):
            return jnp.concatenate(
                [
                    jnp.concatenate(
                        [recv[j, t, :, 2 * kp + b].astype(F32).reshape(128, 128) for t in tiles],
                        axis=0,
                    )
                    for b in range(2)
                ],
                axis=1,
            ).astype(BF)

        def leave(kp, t, value):
            for b in range(2):
                part = value[:, 128 * b : 128 * (b + 1)].reshape(S, 8, 128)
                back[j, t, :, 2 * kp + b] = part.astype(BF)

        def ship(t):
            m = modes(t)
            home[j, t, pl.ds(me * L, m)] = back[j, t, me, pl.ds(0, m)]

            @pl.loop(1, S)
            def _(k):
                d = lax.rem(me + k, S)
                remote(
                    back.at[j, t, d, pl.ds(0, m)], home.at[j, t, pl.ds(me * L, m)], 2 + j, t, d
                ).start()

        def low_modes(kp, tiles):
            k = 128 * len(tiles)
            spectrum = fold(dot(trf[:, :k], load(kp, tiles))) * kern[1, kp]
            high, low = halves(spectrum)
            w = dot(tri[0, :k], high) + dot(tri[1, :k], high) + dot(tri[0, :k], low)
            left_over = w - w.astype(BF).astype(F32)
            e = lax.broadcasted_iota(jnp.int32, (128, 256), 0) & 7
            leave(kp, 5, w[:128])
            leave(kp, 6, jnp.where(e < 2, w[128:256], left_over[128:256]))
            if len(tiles) == 3:
                leave(kp, 7, left_over[256:])

        for t in range(B + 1, TILES):
            arrived(j, t)
        low_modes(0, (5, 6, 7))

        @pl.loop(1, L // 2)
        def _(kp):
            low_modes(kp, (5, 6))

        for t in range(B + 1, TILES):
            ship(t)
        arrived(j, 0)
        carry[...] = jnp.zeros((L // 2, 128, 256), F32)

        @pl.loop(0, B)
        def _(i):
            arrived(j, i + 1)

            @pl.loop(0, L // 2)
            def _(kp):
                spectrum = fold(dot(tzf[i], load(kp, (i, i + 1)))) * kern[0, kp]
                high, low = halves(spectrum)
                w = dot(tzi[0, i], high) + dot(tzi[1, i], high) + dot(tzi[0, i], low)
                leave(kp, i, carry[kp] + w[:128])
                carry[kp] = w[128:]

            ship(i)

        @pl.loop(0, L // 2)
        def _(kp):
            leave(kp, B, carry[kp])

        ship(B)

    def inverse(j):
        def unstage(t):
            m = modes(t)

            @pl.loop(0, S)
            def _(c):
                block = home[j, t, pl.ds(c * L, m)].astype(F32)
                stage[t, pl.ds(c * 8 * L, 8 * m)] = block.reshape(8 * m, 128)

        def planes(row):
            got = []
            for b in range(2):
                t, at = place(row + b)
                got.append(stage[t, at, :])
            return jnp.concatenate(got, axis=1).astype(BF)

        stage[TILES - 1] = jnp.zeros((8 * N, 128), F32)
        for t in range(B + 1, TILES):
            returned(j, t)
            unstage(t)

        @pl.loop(0, L // 2)
        def _(zz):
            row = B * L + 2 * zz
            low_y = fold(dot(txi[...], planes(row))) + dot(txi[:N], planes(row + L))
            for h, part in enumerate(halves(low_y)):
                for b in range(2):
                    rest_parts[h, 2 * zz + b] = part[:, 128 * b : 128 * (b + 1)]

        returned(j, 0)
        unstage(0)

        @pl.loop(0, B)
        def _(i):
            returned(j, i + 1)
            unstage(i + 1)

            @pl.loop(0, L // 2)
            def _(zz):
                two = pl.ds(2 * zz, 2)
                main = halves(fold(dot(txi[...], planes(i * L + 2 * zz))))
                high, low = (
                    jnp.concatenate(
                        [
                            jnp.concatenate(
                                [main[h][:, 128 * b : 128 * (b + 1)], rest_parts[h, 2 * zz + b]],
                                axis=1,
                            )
                            for b in range(2)
                        ],
                        axis=0,
                    )
                    for h in range(2)
                )
                v = dot(high, tyi[0, i]) + dot(low, tyi[0, i]) + dot(high, tyi[1, i])
                v = v.reshape(2, N, N) * par[j, two]
                if j == 0:
                    total[i, two] = v
                else:
                    out[i, two] = (-0.25 * (total[i, two] + v)).astype(BF)

    first = owner[0] == last
    index_a = jnp.where(first, index[0], index[1])
    index_b = jnp.where(first, index[1], index[0])
    owner_b = jnp.where(first, owner[1], owner[0])
    others = gathered.at[0, pl.ds(0, (bands - 1) * CH)]
    ring = bands // 2
    wide = 2 * CH
    most = gathered.at[1, pl.ds(0, (ring - 1) * wide)]
    along = lax.rem(band, ring)
    start = band - along
    loads[0].wait()

    @pl.when(band == last)
    def _():
        pick(chosen, [jnp.where(index_a == i, 1.0, 0.0) for i in range(B)])

    pl.semaphore_wait(barrier, S + bands - 2)

    @pl.when(band == last)
    def _():
        @pl.loop(1, bands)
        def _(k):
            c = lax.rem(band + k, bands)
            share(chosen.at[chunk(c)], gathered.at[0, chunk(c)], 0, c).start()

        gathered[0, chunk(last)] = chosen[chunk(last)]

    is_b = owner_b == band
    pick(masked, [jnp.where((index_b == i) & is_b, 1.0, 0.0) for i in range(B)])

    @pl.when(band != last)
    def _():
        mine = gathered.at[0, chunk(band)]
        share(mine, mine, 0, 0).wait_recv()

    @pl.loop(1, bands)
    def _(k):
        mine = gathered.at[0, chunk(band)]
        share(mine, mine, 1, lax.rem(band + k, bands)).start()

    coulomb()
    share(others, others, 1, 0).wait_recv()

    @pl.loop(1, ring)
    def _(k):
        c = lax.rem(along + k, ring)
        share(masked.at[block(c)], heap.at[along], 2, start + c).start()

    unpack(0)
    for load in loads[1:]:
        load.wait()

    def reduce_b():
        share(most, most, 2, 0).wait_recv()
        heap[along] = masked[block(along)]
        whole = heap[0].astype(F32)
        for s in range(1, ring):
            whole = whole + heap[s].astype(F32)
        part_b[...] = whole.astype(BF)
        share(part_b, other_b, 3, lax.rem(band + ring, bands)).start()

    def gather_b():
        share(part_b, other_b, 3, 0).wait_recv()
        whole = part_b[...].astype(F32) + other_b[...].astype(F32)
        mine = gathered.at[1, block(along)]
        mine[...] = whole.astype(BF)

        @pl.loop(1, ring)
        def _(k):
            share(mine, mine, 4, start + lax.rem(along + k, ring)).start()

    stage[TILES - 1] = jnp.zeros((8 * N, 128), F32)
    forward(0, (reduce_b, gather_b))
    share(most, most, 4, 0).wait_recv()
    unpack(1)
    forward(1, ())
    for j in range(2):
        middle(j)
    for j in range(2):
        inverse(j)
    for j in range(2):
        for t in range(TILES):
            sent = recv.at[j, t, pl.ds(0, S - 1), pl.ds(0, modes(t))]
            remote(sent, sent, j, t, 0).wait_send()
            remote(sent, sent, 2 + j, t, 0).wait_send()
    share(others, others, 1, 0).wait_send()
    share(most, most, 2, 0).wait_send()
    share(part_b, part_b, 3, 0).wait_send()
    share(most, most, 4, 0).wait_send()

    @pl.when(band == last)
    def _():
        share(others, others, 0, 0).wait_send()


def solve(orbitals, owner, index):
    tables = [jnp.asarray(t) for t in make_tables()]
    vmem = pl.BlockSpec(memory_space=pltpu.VMEM)
    smem = pl.BlockSpec(memory_space=pltpu.SMEM)
    hbm = pl.BlockSpec(memory_space=pl.ANY)
    bands = lax.axis_size("band")
    return pl.pallas_call(
        solve_kernel,
        out_shape=jax.ShapeDtypeStruct(orbitals.shape, BF),
        in_specs=[smem, smem] + [hbm] * (1 + len(tables)),
        out_specs=vmem,
        scratch_shapes=[pltpu.VMEM(orbitals.shape, BF)]
        + [pltpu.VMEM(t.shape, BF) for t in tables]
        + [
            pltpu.VMEM((bands * CH, 128), BF),
            pltpu.VMEM((bands * CH, 128), BF),
            pltpu.VMEM((bands // 2, 2 * CH, 128), BF),
            pltpu.VMEM((2 * CH, 128), BF),
            pltpu.VMEM((2 * CH, 128), BF),
            pltpu.VMEM((2, bands * CH, 128), BF),
            pltpu.VMEM((2, L, N, N), F32),
            pltpu.VMEM((2, TILES, N, 8, 128), BF),
            pltpu.VMEM((2, TILES, S, L, 8, 128), BF),
            pltpu.VMEM((2, TILES, S, L, 8, 128), BF),
            pltpu.VMEM((2, TILES, N, 8, 128), BF),
            pltpu.VMEM((TILES, 8 * N, 128), F32),
            pltpu.VMEM((L, N, 128), F32),
            pltpu.VMEM((2, L, N, 128), BF),
            pltpu.VMEM((L // 2, 128, 256), F32),
            pltpu.VMEM((B, L, N, N), F32),
            pltpu.VMEM((2, L // 2, N, 256), F32),
            pltpu.SemaphoreType.DMA((1 + len(tables),)),
            pltpu.SemaphoreType.DMA((4, TILES)),
            pltpu.SemaphoreType.DMA((4, TILES)),
            pltpu.SemaphoreType.DMA((5,)),
            pltpu.SemaphoreType.DMA((5,)),
        ],
        compiler_params=pltpu.CompilerParams(
            collective_id=0, has_side_effects=True, vmem_limit_bytes=60 << 20
        ),
        name="solve_pairs",
    )(owner, index, orbitals, *tables)


def per_device(orbitals, owner, index):
    return solve(orbitals, owner, index)


def solution(mesh):
    placed = (P("band", "slab", None, None), P(), P())
    return jax.shard_map(
        per_device,
        mesh=mesh,
        in_specs=placed,
        out_specs=P("band", "slab", None, None),
        check_vma=False,
    )
```

```python
import math

import jax
import jax.numpy as jnp
import ml_dtypes
import numpy as np
from jax import lax
from jax.experimental import pallas as pl
from jax.experimental.pallas import tpu as pltpu
from jax.sharding import PartitionSpec as P

spacing = 0.293125
MESH = pl.DeviceIdType.MESH
CH = 128
BF = jnp.bfloat16
F32 = jnp.float32
N = 160
S = 16
L = N // S
B = 4
LOW = 32
TILES = 6
EXTRA = 6


def split_table(table):
    high = table.astype(ml_dtypes.bfloat16)
    low = (table - high.astype(np.float64)).astype(ml_dtypes.bfloat16)
    return high, low


def make_tables():
    steps = np.arange(N)
    angle = 2.0 * np.pi / N * (steps[:, None] * steps[None, :] % N)
    cas = np.cos(angle) + np.sin(angle)
    by_size = np.array([(c + 1) // 2 if c % 2 else (N - c // 2) % N for c in range(N)])
    along_y = cas[by_size]
    ty = np.zeros((B, N, 256))
    for q in range(B):
        ty[q, :, :128] = along_y[LOW:].T
        ty[q, :, 128 + LOW * q : 128 + LOW * (q + 1)] = along_y[:LOW].T
    rows = np.array([by_size[(r % L) * S + r // L] for r in range(N)])
    tx = cas[rows]
    tz = np.zeros((B, N, 2, S, 8))
    for i in range(B):
        for h in range(2):
            for e in range(8):
                z = 8 * (i + h) + e - L * i
                if 0 <= z < L:
                    for s in range(S):
                        tz[i, :, h, s, e] = cas[:, s * L + z]
    tl = np.zeros((4, N, 2, S, 8))
    for v in range(4):
        for s in range(S):
            tl[v, :, 0, s] = cas[:, s * L : s * L + 8]
            tl[v, :, 1, s, v] = cas[:, s * L + 8]
            tl[v, :, 1, s, 4 + v] = cas[:, s * L + 9]
    tz = tz.reshape(B, N, 256)
    tl = tl.reshape(4, N, 256)
    stack = lambda t, axis: np.concatenate(split_table(t), axis=axis)
    pair = lambda t: np.stack(split_table(t))
    return pair(ty), stack(tx, 0), stack(tx.T, 0), stack(tz, 1), stack(tl, 1)


def dot(a, b):
    return jnp.dot(a, b, preferred_element_type=F32)


def halves(value):
    high = value.astype(BF)
    return high, (value - high.astype(F32)).astype(BF)


def fold(both):
    return both[:N] + both[N:]


def left(table, value):
    high, low = halves(value)
    return fold(dot(table, high)) + dot(table[:N], low)


def solve_kernel(
    owner, index, orbitals, *refs
):
    tables, out, phi = refs[:5], refs[5], refs[6]
    tyf, txf, txi, tzf, tlf = held = refs[7:12]
    (
        tyi, tzi, tli, chosen, masked, heap, part_b, other_b, gathered, par,
        send, recv, back, home, send_x, recv_x, back_x, home_x,
        stage, extra, extra_sum, rest, rest_parts, carry, total, kern,
        load_sem, send_sem, recv_sem, share_send, share_recv,
    ) = refs[12:]
    loads = [
        pltpu.make_async_copy(src, dst, load_sem.at[n])
        for n, (src, dst) in enumerate(zip((orbitals,) + tables, (phi,) + held))
    ]
    for load in loads:
        load.start()
    me = lax.axis_index("slab")
    band = lax.axis_index("band")
    bands = lax.axis_size("band")
    last = bands - 1
    barrier = pltpu.get_barrier_semaphore()

    @pl.loop(1, S)
    def _(k):
        pl.semaphore_signal(
            barrier, inc=1, device_id={"slab": lax.rem(me + k, S)}, device_id_type=MESH
        )

    @pl.loop(1, bands)
    def _(k):
        pl.semaphore_signal(
            barrier, inc=1, device_id={"band": lax.rem(band + k, bands)}, device_id_type=MESH
        )

    def remote(src, dst, which, t, d):
        return pltpu.make_async_remote_copy(
            src_ref=src,
            dst_ref=dst,
            send_sem=send_sem.at[which, t],
            recv_sem=recv_sem.at[which, t],
            device_id={"slab": d},
            device_id_type=MESH,
        )

    def share(src, dst, which, d):
        return pltpu.make_async_remote_copy(
            src_ref=src,
            dst_ref=dst,
            send_sem=share_send.at[which],
            recv_sem=share_recv.at[which],
            device_id={"band": d},
            device_id_type=MESH,
        )

    def chunk(c):
        return pl.ds(pl.multiple_of(c * CH, CH), CH)

    def block(c):
        return pl.ds(pl.multiple_of(c * 2 * CH, 2 * CH), 2 * CH)

    def pick(flat, weights):
        flat[pl.ds(N * L * 5 // 4, 48)] = jnp.zeros((48, 128), BF)

        @pl.loop(0, L // 2)
        def _(zz):
            two = pl.ds(2 * zz, 2)
            plane = phi[0, two].astype(F32) * weights[0]
            for i in range(1, B):
                plane = plane + phi[i, two].astype(F32) * weights[i]
            flat[pl.ds(pl.multiple_of(2 * N * zz, 2 * N), 2 * N)] = (
                plane[:, :, :128].reshape(2 * N, 128).astype(BF)
            )
            tail = [
                jnp.concatenate([plane[b, 40 * q : 40 * q + 40, 128:] for q in range(4)], axis=1)
                for b in range(2)
            ]
            flat[pl.ds(pl.multiple_of(N * L + 80 * zz, 80), 80)] = (
                jnp.concatenate(tail, axis=0).astype(BF)
            )

    def unpack(j):
        @pl.loop(0, L // 2)
        def _(zz):
            main = gathered[j, pl.ds(pl.multiple_of(2 * N * zz, 2 * N), 2 * N)].astype(F32)
            par[j, pl.ds(2 * zz, 2), :, :128] = main.reshape(2, N, 128)
            tail = gathered[j, pl.ds(pl.multiple_of(N * L + 80 * zz, 80), 80)].astype(F32)
            for b in range(2):
                for q in range(4):
                    par[j, 2 * zz + b, 40 * q : 40 * q + 40, 128:] = tail[
                        40 * b : 40 * b + 40, 32 * q : 32 * q + 32
                    ]

    def coulomb():
        scale = (2.0 * math.pi / (N * spacing)) ** 2
        size = 4.0 * math.pi / (scale * N**3)
        z = lax.broadcasted_iota(jnp.int32, (N, 256), 0)
        lane = lax.broadcasted_iota(jnp.int32, (N, 256), 1)
        z = jnp.minimum(z, N - z)
        second = lane >> 7
        lane = lane & 127

        @pl.loop(0, L // 2)
        def _(kp):
            x = ((2 * kp + second) * S + me + 1) >> 1
            for u, y in enumerate(((lane + LOW + 1) >> 1, ((lane & (LOW - 1)) + 1) >> 1)):
                g = (z * z + x * x + y * y).astype(F32)
                kern[u, kp] = jnp.where(g > 0, size / jnp.where(g > 0, g, 1.0), 0.0)

    def place(row):
        return lax.div(row, 8), pl.ds(lax.rem(row, 8), N, stride=8)

    def turn_tables():
        for h in range(2):
            for i in range(B):
                tyi[h, i] = tyf[h, i].astype(F32).T.astype(BF)
                tzi[h, i] = tzf[i, N * h : N * (h + 1)].astype(F32).T.astype(BF)
                tli[h, i] = tlf[i, N * h : N * (h + 1)].astype(F32).T.astype(BF)

    def flush(j, t):
        @pl.loop(0, S)
        def _(d):
            block = stage[t, pl.ds(d * 8 * L, 8 * L)].reshape(L, 8, 128)
            send[j, t, pl.ds(d * L, L)] = block.astype(BF)

        recv[j, t, me] = send[j, t, pl.ds(me * L, L)]

        @pl.loop(1, S)
        def _(k):
            d = lax.rem(me + k, S)
            remote(send.at[j, t, pl.ds(d * L, L)], recv.at[j, t, me], j, t, d).start()

    def each_extra(d, move):
        base = d * 8 * L
        for o in range(2):
            for b in range(2):
                move((d, o, slice(4 * b, 4 * b + 4)), (6, pl.ds(base + 8 * o + b, 4, stride=16)))
                move((d, 2 + o, pl.ds(4 * b, 1)), (6, pl.ds(base + 64 + 8 * o + b, 1)))
                move((d, 2 + o, pl.ds(4 * b + 1, 1)), (6, pl.ds(base + 8 * o + 2 + b, 1)))
            move((d, 4 + o), (7, pl.ds(base + 8 * o, 8)))

    def flush_extra(j):
        @pl.loop(0, S)
        def _(d):
            def move(to, source):
                extra[to] = stage[source]

            each_extra(d, move)
            send_x[j, d] = extra[d].astype(BF)

        recv_x[j, me] = send_x[j, me]

        @pl.loop(1, S)
        def _(k):
            d = lax.rem(me + k, S)
            remote(send_x.at[j, d], recv_x.at[j, me], j, TILES, d).start()

    def residual_row(zz):
        return 2 * zz + jnp.where(zz < 4, 56, 42)

    def forward(j, between):
        rest[...] = jnp.zeros((L, N, 128), F32)

        @pl.loop(0, B)
        def _(i):
            @pl.loop(0, L // 2)
            def _(zz):
                two = pl.ds(2 * zz, 2)
                density = phi[i, two].astype(F32) * par[j, two]
                high, low = halves(density.reshape(2 * N, N))
                y = dot(high, tyf[0, i]) + dot(low, tyf[0, i]) + dot(high, tyf[1, i])
                rest[two] += y[:, 128:].reshape(2, N, 128)
                main = jnp.concatenate([y[:N, :128], y[N:, :128]], axis=1)
                x = left(txf[...], main)
                for b in range(2):
                    t, at = place(i * L + 2 * zz + b)
                    stage[t, at, :] = x[:, 128 * b : 128 * (b + 1)]

            flush(j, i)
            for n, step in enumerate(between):
                pl.when(i == n + 1)(step)

        flush(j, B)

        @pl.loop(0, L // 2)
        def _(zz):
            low = jnp.concatenate([rest[2 * zz], rest[2 * zz + 1]], axis=1)
            x = left(txf[...], low)
            left_over = x - x.astype(BF).astype(F32)
            for b in range(2):
                t, at = place(B * L + 2 * zz + b)
                stage[t, at, :] = x[:, 128 * b : 128 * (b + 1)]
                t, at = place(residual_row(zz) + b)
                stage[t, at, :] = left_over[:, 128 * b : 128 * (b + 1)]

        flush(j, B + 1)
        flush_extra(j)

    def arrived(j, t):
        others = recv.at[j, t, pl.ds(0, S - 1)]
        remote(others, others, j, t, 0).wait_recv()

    def returned(j, t):
        others = recv.at[j, t, pl.ds(0, S - 1)]
        remote(others, others, 2 + j, t, 0).wait_recv()

    others_x = recv_x.at[0, pl.ds(0, S - 1)]

    def middle(j):
        def load(pieces):
            return jnp.concatenate(
                [
                    jnp.concatenate(
                        [piece(b).astype(F32).reshape(128, 128) for piece in pieces], axis=0
                    )
                    for b in range(2)
                ],
                axis=1,
            ).astype(BF)

        def tile(kp, t):
            return lambda b: recv[j, t, :, 2 * kp + b]

        def extra_tile(t):
            return lambda b: recv_x[j, :, t + b]

        def parts(value):
            for b in range(2):
                yield b, value[:, 128 * b : 128 * (b + 1)].reshape(S, 8, 128).astype(BF)

        def leave(kp, t, value):
            for b, part in parts(value):
                back[j, t, :, 2 * kp + b] = part

        def leave_extra(t, value):
            for b, part in parts(value):
                back_x[j, :, t + b] = part

        def ship(t):
            home[j, t, pl.ds(me * L, L)] = back[j, t, me]

            @pl.loop(1, S)
            def _(k):
                d = lax.rem(me + k, S)
                remote(back.at[j, t, d], home.at[j, t, pl.ds(me * L, L)], 2 + j, t, d).start()

        def apply(table, spectrum):
            high, low = halves(spectrum)
            return dot(table(0), high) + dot(table(1), high) + dot(table(0), low)

        def low_modes(kp, v, t, residual):
            spectrum = fold(dot(tlf[v], load((tile(kp, B + 1), extra_tile(t)))))
            if residual:
                spectrum += fold(dot(tlf[1], load((extra_tile(4), extra_tile(2)))))
            spectrum *= kern[1, kp]
            w = apply(lambda h: tli[h, v], spectrum)
            leave(kp, B + 1, w[:128])
            if residual:
                r = apply(lambda h: tli[h, 1], spectrum)
                r -= r.astype(BF).astype(F32)
                leave_extra(4, r[:128])
                extra_sum[1] = r[128:]
            return w[128:]

        arrived(j, B + 1)
        remote(others_x, others_x, j, TILES, 0).wait_recv()
        extra_sum[0] = low_modes(0, 0, 0, True)

        @pl.loop(1, 4)
        def _(kp):
            extra_sum[0] += low_modes(kp, kp, 0, False)

        extra_sum[1] += low_modes(4, 0, 2, False)
        for n in range(2):
            leave_extra(2 * n, extra_sum[n])
        ship(B + 1)
        home_x[j, me] = back_x[j, me]

        @pl.loop(1, S)
        def _(k):
            d = lax.rem(me + k, S)
            remote(back_x.at[j, d], home_x.at[j, me], 2 + j, TILES, d).start()

        arrived(j, 0)
        carry[...] = jnp.zeros((L // 2, 128, 256), F32)

        @pl.loop(0, B)
        def _(i):
            arrived(j, i + 1)

            @pl.loop(0, L // 2)
            def _(kp):
                spectrum = fold(dot(tzf[i], load((tile(kp, i), tile(kp, i + 1)))))
                w = apply(lambda h: tzi[h, i], spectrum * kern[0, kp])
                leave(kp, i, carry[kp] + w[:128])
                carry[kp] = w[128:]

            ship(i)

        @pl.loop(0, L // 2)
        def _(kp):
            leave(kp, B, carry[kp])

        ship(B)

    def inverse(j):
        def unstage(t):
            @pl.loop(0, S)
            def _(c):
                block = home[j, t, pl.ds(c * L, L)].astype(F32)
                stage[t, pl.ds(c * 8 * L, 8 * L)] = block.reshape(8 * L, 128)

        def planes(row):
            got = []
            for b in range(2):
                t, at = place(row + b)
                got.append(stage[t, at, :])
            return jnp.concatenate(got, axis=1).astype(BF)

        returned(j, B + 1)
        unstage(B + 1)
        for t in (6, 7):
            stage[t] = jnp.zeros((8 * N, 128), F32)
        remote(others_x, others_x, 2 + j, TILES, 0).wait_recv()

        @pl.loop(0, S)
        def _(d):
            extra[d] = home_x[j, d].astype(F32)

            def move(source, to):
                stage[to] = extra[source]

            each_extra(d, move)

        @pl.loop(0, L // 2)
        def _(zz):
            low_y = fold(dot(txi[...], planes(B * L + 2 * zz)))
            low_y += dot(txi[:N], planes(residual_row(zz)))
            for h, part in enumerate(halves(low_y)):
                for b in range(2):
                    rest_parts[h, 2 * zz + b] = part[:, 128 * b : 128 * (b + 1)]

        returned(j, 0)
        unstage(0)

        @pl.loop(0, B)
        def _(i):
            returned(j, i + 1)
            unstage(i + 1)

            @pl.loop(0, L // 2)
            def _(zz):
                two = pl.ds(2 * zz, 2)
                main = halves(fold(dot(txi[...], planes(i * L + 2 * zz))))
                high, low = (
                    jnp.concatenate(
                        [
                            jnp.concatenate(
                                [main[h][:, 128 * b : 128 * (b + 1)], rest_parts[h, 2 * zz + b]],
                                axis=1,
                            )
                            for b in range(2)
                        ],
                        axis=0,
                    )
                    for h in range(2)
                )
                v = dot(high, tyi[0, i]) + dot(low, tyi[0, i]) + dot(high, tyi[1, i])
                v = v.reshape(2, N, N) * par[j, two]
                if j == 0:
                    total[i, two] = v
                else:
                    out[i, two] = (-0.25 * (total[i, two] + v)).astype(BF)

    first = owner[0] == last
    index_a = jnp.where(first, index[0], index[1])
    index_b = jnp.where(first, index[1], index[0])
    owner_b = jnp.where(first, owner[1], owner[0])
    others = gathered.at[0, pl.ds(0, (bands - 1) * CH)]
    ring = bands // 2
    wide = 2 * CH
    most = gathered.at[1, pl.ds(0, (ring - 1) * wide)]
    along = lax.rem(band, ring)
    start = band - along
    loads[0].wait()

    @pl.when(band == last)
    def _():
        pick(chosen, [jnp.where(index_a == i, 1.0, 0.0) for i in range(B)])

    pl.semaphore_wait(barrier, S + bands - 2)

    @pl.when(band == last)
    def _():
        @pl.loop(1, bands)
        def _(k):
            c = lax.rem(band + k, bands)
            share(chosen.at[chunk(c)], gathered.at[0, chunk(c)], 0, c).start()

        gathered[0, chunk(last)] = chosen[chunk(last)]

    is_b = owner_b == band
    pick(masked, [jnp.where((index_b == i) & is_b, 1.0, 0.0) for i in range(B)])

    @pl.when(band != last)
    def _():
        mine = gathered.at[0, chunk(band)]
        share(mine, mine, 0, 0).wait_recv()

    @pl.loop(1, bands)
    def _(k):
        mine = gathered.at[0, chunk(band)]
        share(mine, mine, 1, lax.rem(band + k, bands)).start()

    coulomb()
    for load in loads[1:]:
        load.wait()
    turn_tables()
    share(others, others, 1, 0).wait_recv()

    @pl.loop(1, ring)
    def _(k):
        c = lax.rem(along + k, ring)
        share(masked.at[block(c)], heap.at[along], 2, start + c).start()

    unpack(0)

    def reduce_b():
        share(most, most, 2, 0).wait_recv()
        heap[along] = masked[block(along)]
        whole = heap[0].astype(F32)
        for s in range(1, ring):
            whole = whole + heap[s].astype(F32)
        part_b[...] = whole.astype(BF)
        share(part_b, other_b, 3, lax.rem(band + ring, bands)).start()

    def gather_b():
        share(part_b, other_b, 3, 0).wait_recv()
        whole = part_b[...].astype(F32) + other_b[...].astype(F32)
        mine = gathered.at[1, block(along)]
        mine[...] = whole.astype(BF)

        @pl.loop(1, ring)
        def _(k):
            share(mine, mine, 4, start + lax.rem(along + k, ring)).start()

    extra[...] = jnp.zeros((S, EXTRA, 8, 128), F32)
    forward(0, (reduce_b, gather_b))
    share(most, most, 4, 0).wait_recv()
    unpack(1)
    forward(1, ())
    for j in range(2):
        middle(j)
    for j in range(2):
        inverse(j)
    for j in range(2):
        for t in range(TILES):
            sent = recv.at[j, t, pl.ds(0, S - 1)]
            remote(sent, sent, j, t, 0).wait_send()
            remote(sent, sent, 2 + j, t, 0).wait_send()
        remote(others_x, others_x, j, TILES, 0).wait_send()
        remote(others_x, others_x, 2 + j, TILES, 0).wait_send()
    share(others, others, 1, 0).wait_send()
    share(most, most, 2, 0).wait_send()
    share(part_b, part_b, 3, 0).wait_send()
    share(most, most, 4, 0).wait_send()

    @pl.when(band == last)
    def _():
        share(others, others, 0, 0).wait_send()


def solve(orbitals, owner, index):
    tables = [jnp.asarray(t) for t in make_tables()]
    vmem = pl.BlockSpec(memory_space=pltpu.VMEM)
    smem = pl.BlockSpec(memory_space=pltpu.SMEM)
    hbm = pl.BlockSpec(memory_space=pl.ANY)
    bands = lax.axis_size("band")
    return pl.pallas_call(
        solve_kernel,
        out_shape=jax.ShapeDtypeStruct(orbitals.shape, BF),
        in_specs=[smem, smem] + [hbm] * (1 + len(tables)),
        out_specs=vmem,
        scratch_shapes=[pltpu.VMEM(orbitals.shape, BF)]
        + [pltpu.VMEM(t.shape, BF) for t in tables]
        + [
            pltpu.VMEM((2, B, 256, N), BF),
            pltpu.VMEM((2, B, 256, N), BF),
            pltpu.VMEM((2, 4, 256, N), BF),
            pltpu.VMEM((bands * CH, 128), BF),
            pltpu.VMEM((bands * CH, 128), BF),
            pltpu.VMEM((bands // 2, 2 * CH, 128), BF),
            pltpu.VMEM((2 * CH, 128), BF),
            pltpu.VMEM((2 * CH, 128), BF),
            pltpu.VMEM((2, bands * CH, 128), BF),
            pltpu.VMEM((2, L, N, N), F32),
            pltpu.VMEM((2, TILES, N, 8, 128), BF),
            pltpu.VMEM((2, TILES, S, L, 8, 128), BF),
            pltpu.VMEM((2, TILES, S, L, 8, 128), BF),
            pltpu.VMEM((2, TILES, N, 8, 128), BF),
            pltpu.VMEM((2, S, EXTRA, 8, 128), BF),
            pltpu.VMEM((2, S, EXTRA, 8, 128), BF),
            pltpu.VMEM((2, S, EXTRA, 8, 128), BF),
            pltpu.VMEM((2, S, EXTRA, 8, 128), BF),
            pltpu.VMEM((8, 8 * N, 128), F32),
            pltpu.VMEM((S, EXTRA, 8, 128), F32),
            pltpu.VMEM((2, 128, 256), F32),
            pltpu.VMEM((L, N, 128), F32),
            pltpu.VMEM((2, L, N, 128), BF),
            pltpu.VMEM((L // 2, 128, 256), F32),
            pltpu.VMEM((B, L, N, N), F32),
            pltpu.VMEM((2, L // 2, N, 256), F32),
            pltpu.SemaphoreType.DMA((1 + len(tables),)),
            pltpu.SemaphoreType.DMA((4, TILES + 1)),
            pltpu.SemaphoreType.DMA((4, TILES + 1)),
            pltpu.SemaphoreType.DMA((5,)),
            pltpu.SemaphoreType.DMA((5,)),
        ],
        compiler_params=pltpu.CompilerParams(
            collective_id=0, has_side_effects=True, vmem_limit_bytes=60 << 20
        ),
        name="solve_pairs",
    )(owner, index, orbitals, *tables)


def per_device(orbitals, owner, index):
    return solve(orbitals, owner, index)


def solution(mesh):
    placed = (P("band", "slab", None, None), P(), P())
    return jax.shard_map(
        per_device,
        mesh=mesh,
        in_specs=placed,
        out_specs=P("band", "slab", None, None),
        check_vma=False,
    )
```

```python
import math

import jax
import jax.numpy as jnp
import ml_dtypes
import numpy as np
from jax import lax
from jax.experimental import pallas as pl
from jax.experimental.pallas import tpu as pltpu
from jax.sharding import PartitionSpec as P

spacing = 0.293125
MESH = pl.DeviceIdType.MESH
CH = 128
BF = jnp.bfloat16
F32 = jnp.float32
N = 160
S = 16
L = N // S
B = 4
LOW = 32
TILES = 6
EXTRA = 6


def split_table(table):
    high = table.astype(ml_dtypes.bfloat16)
    low = (table - high.astype(np.float64)).astype(ml_dtypes.bfloat16)
    return high, low


def make_tables():
    steps = np.arange(N)
    angle = 2.0 * np.pi / N * (steps[:, None] * steps[None, :] % N)
    cas = np.cos(angle) + np.sin(angle)
    by_size = np.array([(c + 1) // 2 if c % 2 else (N - c // 2) % N for c in range(N)])
    along_y = cas[by_size]
    ty = np.zeros((B, N, 256))
    for q in range(B):
        ty[q, :, :128] = along_y[LOW:].T
        ty[q, :, 128 + LOW * q : 128 + LOW * (q + 1)] = along_y[:LOW].T
    rows = np.array([by_size[(r % L) * S + r // L] for r in range(N)])
    tx = cas[rows]
    tz = np.zeros((B, N, 2, S, 8))
    for i in range(B):
        for h in range(2):
            for e in range(8):
                z = 8 * (i + h) + e - L * i
                if 0 <= z < L:
                    for s in range(S):
                        tz[i, :, h, s, e] = cas[:, s * L + z]
    tl = np.zeros((4, N, 2, S, 8))
    for v in range(4):
        for s in range(S):
            tl[v, :, 0, s] = cas[:, s * L : s * L + 8]
            tl[v, :, 1, s, v] = cas[:, s * L + 8]
            tl[v, :, 1, s, 4 + v] = cas[:, s * L + 9]
    tz = tz.reshape(B, N, 256)
    tl = tl.reshape(4, N, 256)
    stack = lambda t, axis: np.concatenate(split_table(t), axis=axis)
    pair = lambda t: np.stack(split_table(t))
    return pair(ty), stack(tx, 0), stack(tx.T, 0), stack(tz, 1), stack(tl, 1)


def dot(a, b):
    return jnp.dot(a, b, preferred_element_type=F32)


def halves(value):
    high = value.astype(BF)
    return high, (value - high.astype(F32)).astype(BF)


def fold(both):
    return both[:N] + both[N:]


def left(table, value):
    high, low = halves(value)
    return fold(dot(table, high)) + dot(table[:N], low)


def solve_kernel(
    owner, index, orbitals, *refs
):
    tables, result, phi, out = refs[:5], refs[5], refs[6], refs[7]
    tyf, txf, txi, tzf, tlf = held = refs[8:13]
    (
        tyi, tzi, tli, chosen, masked, heap, part_b, other_b, gathered, par,
        send, recv, back, home, send_x, recv_x, back_x, home_x,
        stage, extra, extra_sum, rest, rest_parts, carry, total, kern,
        load_sem, out_sem, send_sem, recv_sem, share_send, share_recv,
    ) = refs[13:]
    loads = [
        pltpu.make_async_copy(src, dst, load_sem.at[n])
        for n, (src, dst) in enumerate(zip((orbitals,) + tables, (phi,) + held))
    ]
    for load in loads:
        load.start()
    me = lax.axis_index("slab")
    band = lax.axis_index("band")
    bands = lax.axis_size("band")
    last = bands - 1
    barrier = pltpu.get_barrier_semaphore()

    @pl.loop(1, S)
    def _(k):
        pl.semaphore_signal(
            barrier, inc=1, device_id={"slab": lax.rem(me + k, S)}, device_id_type=MESH
        )

    @pl.loop(1, bands)
    def _(k):
        pl.semaphore_signal(
            barrier, inc=1, device_id={"band": lax.rem(band + k, bands)}, device_id_type=MESH
        )

    def remote(src, dst, which, t, d):
        return pltpu.make_async_remote_copy(
            src_ref=src,
            dst_ref=dst,
            send_sem=send_sem.at[which, t],
            recv_sem=recv_sem.at[which, t],
            device_id={"slab": d},
            device_id_type=MESH,
        )

    def share(src, dst, which, d):
        return pltpu.make_async_remote_copy(
            src_ref=src,
            dst_ref=dst,
            send_sem=share_send.at[which],
            recv_sem=share_recv.at[which],
            device_id={"band": d},
            device_id_type=MESH,
        )

    def chunk(c):
        return pl.ds(pl.multiple_of(c * CH, CH), CH)

    def block(c):
        return pl.ds(pl.multiple_of(c * 2 * CH, 2 * CH), 2 * CH)

    def pick(flat, weights):
        flat[pl.ds(N * L * 5 // 4, 48)] = jnp.zeros((48, 128), BF)

        @pl.loop(0, L // 2, unroll=True)
        def _(zz):
            two = pl.ds(2 * zz, 2)
            plane = phi[0, two].astype(F32) * weights[0]
            for i in range(1, B):
                plane = plane + phi[i, two].astype(F32) * weights[i]
            flat[pl.ds(pl.multiple_of(2 * N * zz, 2 * N), 2 * N)] = (
                plane[:, :, :128].reshape(2 * N, 128).astype(BF)
            )
            tail = [
                jnp.concatenate([plane[b, 40 * q : 40 * q + 40, 128:] for q in range(4)], axis=1)
                for b in range(2)
            ]
            flat[pl.ds(pl.multiple_of(N * L + 80 * zz, 80), 80)] = (
                jnp.concatenate(tail, axis=0).astype(BF)
            )

    def unpack(j):
        @pl.loop(0, L // 2, unroll=True)
        def _(zz):
            main = gathered[j, pl.ds(pl.multiple_of(2 * N * zz, 2 * N), 2 * N)].astype(F32)
            par[j, pl.ds(2 * zz, 2), :, :128] = main.reshape(2, N, 128)
            tail = gathered[j, pl.ds(pl.multiple_of(N * L + 80 * zz, 80), 80)].astype(F32)
            for b in range(2):
                for q in range(4):
                    par[j, 2 * zz + b, 40 * q : 40 * q + 40, 128:] = tail[
                        40 * b : 40 * b + 40, 32 * q : 32 * q + 32
                    ]

    def coulomb():
        scale = (2.0 * math.pi / (N * spacing)) ** 2
        size = 4.0 * math.pi / (scale * N**3)
        z = lax.broadcasted_iota(jnp.int32, (N, 256), 0)
        lane = lax.broadcasted_iota(jnp.int32, (N, 256), 1)
        z = jnp.minimum(z, N - z)
        second = lane >> 7
        lane = lane & 127

        @pl.loop(0, L // 2, unroll=True)
        def _(kp):
            x = ((2 * kp + second) * S + me + 1) >> 1
            for u, y in enumerate(((lane + LOW + 1) >> 1, ((lane & (LOW - 1)) + 1) >> 1)):
                g = (z * z + x * x + y * y).astype(F32)
                kern[u, kp] = jnp.where(g > 0, size / jnp.where(g > 0, g, 1.0), 0.0)

    def place(row):
        return lax.div(row, 8), pl.ds(lax.rem(row, 8), N, stride=8)

    def turn_tables():
        for h in range(2):
            for i in range(B):
                tyi[h, i] = tyf[h, i].astype(F32).T.astype(BF)
                tzi[h, i] = tzf[i, N * h : N * (h + 1)].astype(F32).T.astype(BF)
                tli[h, i] = tlf[i, N * h : N * (h + 1)].astype(F32).T.astype(BF)

    def flush(j, t):
        @pl.loop(0, S)
        def _(d):
            block = stage[t, pl.ds(d * 8 * L, 8 * L)].reshape(L, 8, 128)
            send[j, t, pl.ds(d * L, L)] = block.astype(BF)

        recv[j, t, me] = send[j, t, pl.ds(me * L, L)]

        @pl.loop(1, S)
        def _(k):
            d = lax.rem(me + k, S)
            remote(send.at[j, t, pl.ds(d * L, L)], recv.at[j, t, me], j, t, d).start()

    def each_extra(d, move):
        base = d * 8 * L
        for o in range(2):
            for b in range(2):
                move((d, o, slice(4 * b, 4 * b + 4)), (6, pl.ds(base + 8 * o + b, 4, stride=16)))
                move((d, 2 + o, pl.ds(4 * b, 1)), (6, pl.ds(base + 64 + 8 * o + b, 1)))
                move((d, 2 + o, pl.ds(4 * b + 1, 1)), (6, pl.ds(base + 8 * o + 2 + b, 1)))
            move((d, 4 + o), (7, pl.ds(base + 8 * o, 8)))

    def flush_extra(j):
        @pl.loop(0, S)
        def _(d):
            def move(to, source):
                extra[to] = stage[source]

            each_extra(d, move)
            send_x[j, d] = extra[d].astype(BF)

        recv_x[j, me] = send_x[j, me]

        @pl.loop(1, S)
        def _(k):
            d = lax.rem(me + k, S)
            remote(send_x.at[j, d], recv_x.at[j, me], j, TILES, d).start()

    def residual_row(zz):
        return 2 * zz + jnp.where(zz < 4, 56, 42)

    def forward(j, between):
        rest[...] = jnp.zeros((L, N, 128), F32)

        @pl.loop(0, B)
        def _(i):
            @pl.loop(0, L // 2, unroll=True)
            def _(zz):
                two = pl.ds(2 * zz, 2)
                density = phi[i, two].astype(F32) * par[j, two]
                high, low = halves(density.reshape(2 * N, N))
                y = dot(high, tyf[0, i]) + dot(low, tyf[0, i]) + dot(high, tyf[1, i])
                rest[two] += y[:, 128:].reshape(2, N, 128)
                main = jnp.concatenate([y[:N, :128], y[N:, :128]], axis=1)
                x = left(txf[...], main)
                for b in range(2):
                    t, at = place(i * L + 2 * zz + b)
                    stage[t, at, :] = x[:, 128 * b : 128 * (b + 1)]

            flush(j, i)
            for n, step in enumerate(between):
                pl.when(i == n + 1)(step)

        flush(j, B)

        @pl.loop(0, L // 2, unroll=True)
        def _(zz):
            low = jnp.concatenate([rest[2 * zz], rest[2 * zz + 1]], axis=1)
            x = left(txf[...], low)
            left_over = x - x.astype(BF).astype(F32)
            for b in range(2):
                t, at = place(B * L + 2 * zz + b)
                stage[t, at, :] = x[:, 128 * b : 128 * (b + 1)]
                t, at = place(residual_row(zz) + b)
                stage[t, at, :] = left_over[:, 128 * b : 128 * (b + 1)]

        flush(j, B + 1)
        flush_extra(j)

    def arrived(j, t):
        others = recv.at[j, t, pl.ds(0, S - 1)]
        remote(others, others, j, t, 0).wait_recv()

    def returned(j, t):
        others = recv.at[j, t, pl.ds(0, S - 1)]
        remote(others, others, 2 + j, t, 0).wait_recv()

    others_x = recv_x.at[0, pl.ds(0, S - 1)]

    def middle(j):
        def load(pieces):
            return jnp.concatenate(
                [
                    jnp.concatenate(
                        [piece(b).astype(F32).reshape(128, 128) for piece in pieces], axis=0
                    )
                    for b in range(2)
                ],
                axis=1,
            ).astype(BF)

        def tile(kp, t):
            return lambda b: recv[j, t, :, 2 * kp + b]

        def extra_tile(t):
            return lambda b: recv_x[j, :, t + b]

        def parts(value):
            for b in range(2):
                yield b, value[:, 128 * b : 128 * (b + 1)].reshape(S, 8, 128).astype(BF)

        def leave(kp, t, value):
            for b, part in parts(value):
                back[j, t, :, 2 * kp + b] = part

        def leave_extra(t, value):
            for b, part in parts(value):
                back_x[j, :, t + b] = part

        def ship(t):
            home[j, t, pl.ds(me * L, L)] = back[j, t, me]

            @pl.loop(1, S)
            def _(k):
                d = lax.rem(me + k, S)
                remote(back.at[j, t, d], home.at[j, t, pl.ds(me * L, L)], 2 + j, t, d).start()

        def apply(table, spectrum):
            high, low = halves(spectrum)
            return dot(table(0), high) + dot(table(1), high) + dot(table(0), low)

        def low_modes(kp, v, t, residual):
            spectrum = fold(dot(tlf[v], load((tile(kp, B + 1), extra_tile(t)))))
            if residual:
                spectrum += fold(dot(tlf[1], load((extra_tile(4), extra_tile(2)))))
            spectrum *= kern[1, kp]
            w = apply(lambda h: tli[h, v], spectrum)
            leave(kp, B + 1, w[:128])
            if residual:
                r = apply(lambda h: tli[h, 1], spectrum)
                r -= r.astype(BF).astype(F32)
                leave_extra(4, r[:128])
                extra_sum[1] = r[128:]
            return w[128:]

        arrived(j, B + 1)
        remote(others_x, others_x, j, TILES, 0).wait_recv()
        extra_sum[0] = low_modes(0, 0, 0, True)

        @pl.loop(1, 4)
        def _(kp):
            extra_sum[0] += low_modes(kp, kp, 0, False)

        extra_sum[1] += low_modes(4, 0, 2, False)
        for n in range(2):
            leave_extra(2 * n, extra_sum[n])
        ship(B + 1)
        home_x[j, me] = back_x[j, me]

        @pl.loop(1, S)
        def _(k):
            d = lax.rem(me + k, S)
            remote(back_x.at[j, d], home_x.at[j, me], 2 + j, TILES, d).start()

        arrived(j, 0)
        carry[...] = jnp.zeros((L // 2, 128, 256), F32)

        @pl.loop(0, B)
        def _(i):
            arrived(j, i + 1)

            @pl.loop(0, L // 2, unroll=True)
            def _(kp):
                spectrum = fold(dot(tzf[i], load((tile(kp, i), tile(kp, i + 1)))))
                w = apply(lambda h: tzi[h, i], spectrum * kern[0, kp])
                leave(kp, i, carry[kp] + w[:128])
                carry[kp] = w[128:]

            ship(i)

        @pl.loop(0, L // 2, unroll=True)
        def _(kp):
            leave(kp, B, carry[kp])

        ship(B)

    def inverse(j):
        def unstage(t):
            @pl.loop(0, S)
            def _(c):
                block = home[j, t, pl.ds(c * L, L)].astype(F32)
                stage[t, pl.ds(c * 8 * L, 8 * L)] = block.reshape(8 * L, 128)

        def planes(row):
            got = []
            for b in range(2):
                t, at = place(row + b)
                got.append(stage[t, at, :])
            return jnp.concatenate(got, axis=1).astype(BF)

        returned(j, B + 1)
        unstage(B + 1)
        for t in (6, 7):
            stage[t] = jnp.zeros((8 * N, 128), F32)
        remote(others_x, others_x, 2 + j, TILES, 0).wait_recv()

        @pl.loop(0, S)
        def _(d):
            extra[d] = home_x[j, d].astype(F32)

            def move(source, to):
                stage[to] = extra[source]

            each_extra(d, move)

        @pl.loop(0, L // 2, unroll=True)
        def _(zz):
            low_y = fold(dot(txi[...], planes(B * L + 2 * zz)))
            low_y += dot(txi[:N], planes(residual_row(zz)))
            for h, part in enumerate(halves(low_y)):
                for b in range(2):
                    rest_parts[h, 2 * zz + b] = part[:, 128 * b : 128 * (b + 1)]

        returned(j, 0)
        unstage(0)

        @pl.loop(0, B)
        def _(i):
            returned(j, i + 1)
            unstage(i + 1)

            @pl.loop(0, L // 2, unroll=True)
            def _(zz):
                two = pl.ds(2 * zz, 2)
                main = halves(fold(dot(txi[...], planes(i * L + 2 * zz))))
                high, low = (
                    jnp.concatenate(
                        [
                            jnp.concatenate(
                                [main[h][:, 128 * b : 128 * (b + 1)], rest_parts[h, 2 * zz + b]],
                                axis=1,
                            )
                            for b in range(2)
                        ],
                        axis=0,
                    )
                    for h in range(2)
                )
                v = dot(high, tyi[0, i]) + dot(low, tyi[0, i]) + dot(high, tyi[1, i])
                v = v.reshape(2, N, N) * par[j, two]
                if j == 0:
                    total[i, two] = v
                else:
                    out[i, two] = (-0.25 * (total[i, two] + v)).astype(BF)

            if j == 1:
                pltpu.make_async_copy(out.at[i], result.at[i], out_sem.at[i]).start()

    first = owner[0] == last
    index_a = jnp.where(first, index[0], index[1])
    index_b = jnp.where(first, index[1], index[0])
    owner_b = jnp.where(first, owner[1], owner[0])
    others = gathered.at[0, pl.ds(0, (bands - 1) * CH)]
    ring = bands // 2
    wide = 2 * CH
    most = gathered.at[1, pl.ds(0, (ring - 1) * wide)]
    along = lax.rem(band, ring)
    start = band - along
    loads[0].wait()

    @pl.when(band == last)
    def _():
        pick(chosen, [jnp.where(index_a == i, 1.0, 0.0) for i in range(B)])

    pl.semaphore_wait(barrier, S + bands - 2)

    @pl.when(band == last)
    def _():
        @pl.loop(1, bands)
        def _(k):
            c = lax.rem(band + k, bands)
            share(chosen.at[chunk(c)], gathered.at[0, chunk(c)], 0, c).start()

        gathered[0, chunk(last)] = chosen[chunk(last)]

    is_b = owner_b == band
    pick(masked, [jnp.where((index_b == i) & is_b, 1.0, 0.0) for i in range(B)])

    @pl.when(band != last)
    def _():
        mine = gathered.at[0, chunk(band)]
        share(mine, mine, 0, 0).wait_recv()

    @pl.loop(1, bands)
    def _(k):
        mine = gathered.at[0, chunk(band)]
        share(mine, mine, 1, lax.rem(band + k, bands)).start()

    @pl.loop(1, ring)
    def _(k):
        c = lax.rem(along + k, ring)
        share(masked.at[block(c)], heap.at[along], 2, start + c).start()

    coulomb()
    for load in loads[1:]:
        load.wait()
    turn_tables()
    share(others, others, 1, 0).wait_recv()

    unpack(0)

    def reduce_b():
        share(most, most, 2, 0).wait_recv()
        heap[along] = masked[block(along)]
        whole = heap[0].astype(F32)
        for s in range(1, ring):
            whole = whole + heap[s].astype(F32)
        part_b[...] = whole.astype(BF)
        share(part_b, other_b, 3, lax.rem(band + ring, bands)).start()

    def gather_b():
        share(part_b, other_b, 3, 0).wait_recv()
        whole = part_b[...].astype(F32) + other_b[...].astype(F32)
        mine = gathered.at[1, block(along)]
        mine[...] = whole.astype(BF)

        @pl.loop(1, ring)
        def _(k):
            share(mine, mine, 4, start + lax.rem(along + k, ring)).start()

    extra[...] = jnp.zeros((S, EXTRA, 8, 128), F32)
    forward(0, (reduce_b, gather_b))
    share(most, most, 4, 0).wait_recv()
    unpack(1)
    forward(1, ())
    for j in range(2):
        middle(j)
    for j in range(2):
        inverse(j)
    for j in range(2):
        for t in range(TILES):
            sent = recv.at[j, t, pl.ds(0, S - 1)]
            remote(sent, sent, j, t, 0).wait_send()
            remote(sent, sent, 2 + j, t, 0).wait_send()
        remote(others_x, others_x, j, TILES, 0).wait_send()
        remote(others_x, others_x, 2 + j, TILES, 0).wait_send()
    for i in range(B):
        pltpu.make_async_copy(out.at[i], result.at[i], out_sem.at[i]).wait()
    share(others, others, 1, 0).wait_send()
    share(most, most, 2, 0).wait_send()
    share(part_b, part_b, 3, 0).wait_send()
    share(most, most, 4, 0).wait_send()

    @pl.when(band == last)
    def _():
        share(others, others, 0, 0).wait_send()


def solve(orbitals, owner, index):
    tables = [jnp.asarray(t) for t in make_tables()]
    smem = pl.BlockSpec(memory_space=pltpu.SMEM)
    hbm = pl.BlockSpec(memory_space=pl.ANY)
    bands = lax.axis_size("band")
    return pl.pallas_call(
        solve_kernel,
        out_shape=jax.ShapeDtypeStruct(orbitals.shape, BF),
        in_specs=[smem, smem] + [hbm] * (1 + len(tables)),
        out_specs=hbm,
        scratch_shapes=[pltpu.VMEM(orbitals.shape, BF)] * 2
        + [pltpu.VMEM(t.shape, BF) for t in tables]
        + [
            pltpu.VMEM((2, B, 256, N), BF),
            pltpu.VMEM((2, B, 256, N), BF),
            pltpu.VMEM((2, 4, 256, N), BF),
            pltpu.VMEM((bands * CH, 128), BF),
            pltpu.VMEM((bands * CH, 128), BF),
            pltpu.VMEM((bands // 2, 2 * CH, 128), BF),
            pltpu.VMEM((2 * CH, 128), BF),
            pltpu.VMEM((2 * CH, 128), BF),
            pltpu.VMEM((2, bands * CH, 128), BF),
            pltpu.VMEM((2, L, N, N), F32),
            pltpu.VMEM((2, TILES, N, 8, 128), BF),
            pltpu.VMEM((2, TILES, S, L, 8, 128), BF),
            pltpu.VMEM((2, TILES, S, L, 8, 128), BF),
            pltpu.VMEM((2, TILES, N, 8, 128), BF),
            pltpu.VMEM((2, S, EXTRA, 8, 128), BF),
            pltpu.VMEM((2, S, EXTRA, 8, 128), BF),
            pltpu.VMEM((2, S, EXTRA, 8, 128), BF),
            pltpu.VMEM((2, S, EXTRA, 8, 128), BF),
            pltpu.VMEM((8, 8 * N, 128), F32),
            pltpu.VMEM((S, EXTRA, 8, 128), F32),
            pltpu.VMEM((2, 128, 256), F32),
            pltpu.VMEM((L, N, 128), F32),
            pltpu.VMEM((2, L, N, 128), BF),
            pltpu.VMEM((L // 2, 128, 256), F32),
            pltpu.VMEM((B, L, N, N), F32),
            pltpu.VMEM((2, L // 2, N, 256), F32),
            pltpu.SemaphoreType.DMA((1 + len(tables),)),
            pltpu.SemaphoreType.DMA((B,)),
            pltpu.SemaphoreType.DMA((4, TILES + 1)),
            pltpu.SemaphoreType.DMA((4, TILES + 1)),
            pltpu.SemaphoreType.DMA((5,)),
            pltpu.SemaphoreType.DMA((5,)),
        ],
        compiler_params=pltpu.CompilerParams(
            collective_id=0, has_side_effects=True, vmem_limit_bytes=60 << 20
        ),
        name="solve_pairs",
    )(owner, index, orbitals, *tables)


def per_device(orbitals, owner, index):
    return solve(orbitals, owner, index)


def solution(mesh):
    placed = (P("band", "slab", None, None), P(), P())
    return jax.shard_map(
        per_device,
        mesh=mesh,
        in_specs=placed,
        out_specs=P("band", "slab", None, None),
        check_vma=False,
    )
```

```python
import math

import jax
import jax.numpy as jnp
import ml_dtypes
import numpy as np
from jax import lax
from jax.experimental import pallas as pl
from jax.experimental.pallas import tpu as pltpu
from jax.sharding import PartitionSpec as P

spacing = 0.293125
MESH = pl.DeviceIdType.MESH
CH = 128
BF = jnp.bfloat16
F32 = jnp.float32
N = 160
S = 16
L = N // S
B = 4
LOW = 32
TILES = 6
EXTRA = 5


def split_table(table):
    high = table.astype(ml_dtypes.bfloat16)
    low = (table - high.astype(np.float64)).astype(ml_dtypes.bfloat16)
    return high, low


def make_tables():
    steps = np.arange(N)
    angle = 2.0 * np.pi / N * (steps[:, None] * steps[None, :] % N)
    cas = np.cos(angle) + np.sin(angle)
    by_size = np.array([(c + 1) // 2 if c % 2 else (N - c // 2) % N for c in range(N)])
    along_y = cas[by_size]
    ty = np.zeros((B, N, 256))
    for q in range(B):
        ty[q, :, :128] = along_y[LOW:].T
        ty[q, :, 128 + LOW * q : 128 + LOW * (q + 1)] = along_y[:LOW].T
    rows = np.array([by_size[(r % L) * S + r // L] for r in range(N)])
    tx = cas[rows]
    tz = np.zeros((B, N, 2, S, 8))
    for i in range(B):
        for h in range(2):
            for e in range(8):
                z = 8 * (i + h) + e - L * i
                if 0 <= z < L:
                    for s in range(S):
                        tz[i, :, h, s, e] = cas[:, s * L + z]
    tl = np.zeros((4, N, 2, S, 8))
    for v in range(4):
        for s in range(S):
            tl[v, :, 0, s] = cas[:, s * L : s * L + 8]
            tl[v, :, 1, s, v] = cas[:, s * L + 8]
            tl[v, :, 1, s, 4 + v] = cas[:, s * L + 9]
    tz = tz.reshape(B, N, 256)
    tl = tl.reshape(4, N, 256)
    stack = lambda t, axis: np.concatenate(split_table(t), axis=axis)
    pair = lambda t: np.stack(split_table(t))
    return pair(ty), stack(tx, 0), stack(tx.T, 0), stack(tz, 1), stack(tl, 1)


def dot(a, b):
    return jnp.dot(a, b, preferred_element_type=F32)


def halves(value):
    high = value.astype(BF)
    return high, (value - high.astype(F32)).astype(BF)


def fold(both):
    return both[:N] + both[N:]


def left(table, value):
    high, low = halves(value)
    return fold(dot(table, high)) + dot(table[:N], low)


def solve_kernel(
    owner, index, orbitals, *refs
):
    tables, result, phi, out = refs[:5], refs[5], refs[6], refs[7]
    tyf, txf, txi, tzf, tlf = held = refs[8:13]
    (
        tyi, tzi, tli, chosen, masked, heap, part_b, other_b, gathered, par,
        send, recv, back, home, send_x, recv_x, back_x, home_x,
        stage, extra, extra_sum, rest, rest_parts, carry, total, kern,
        load_sem, out_sem, send_sem, recv_sem, share_send, share_recv,
    ) = refs[13:]
    loads = [
        pltpu.make_async_copy(src, dst, load_sem.at[n])
        for n, (src, dst) in enumerate(zip((orbitals,) + tables, (phi,) + held))
    ]
    for load in loads:
        load.start()
    me = lax.axis_index("slab")
    band = lax.axis_index("band")
    bands = lax.axis_size("band")
    last = bands - 1
    barrier = pltpu.get_barrier_semaphore()

    @pl.loop(1, S)
    def _(k):
        pl.semaphore_signal(
            barrier, inc=1, device_id={"slab": lax.rem(me + k, S)}, device_id_type=MESH
        )

    @pl.loop(1, bands)
    def _(k):
        pl.semaphore_signal(
            barrier, inc=1, device_id={"band": lax.rem(band + k, bands)}, device_id_type=MESH
        )

    def remote(src, dst, which, t, d):
        return pltpu.make_async_remote_copy(
            src_ref=src,
            dst_ref=dst,
            send_sem=send_sem.at[which, t],
            recv_sem=recv_sem.at[which, t],
            device_id={"slab": d},
            device_id_type=MESH,
        )

    def share(src, dst, which, d):
        return pltpu.make_async_remote_copy(
            src_ref=src,
            dst_ref=dst,
            send_sem=share_send.at[which],
            recv_sem=share_recv.at[which],
            device_id={"band": d},
            device_id_type=MESH,
        )

    def chunk(c):
        return pl.ds(pl.multiple_of(c * CH, CH), CH)

    def block(c):
        return pl.ds(pl.multiple_of(c * 2 * CH, 2 * CH), 2 * CH)

    def pick(flat, weights):
        flat[pl.ds(N * L * 5 // 4, 48)] = jnp.zeros((48, 128), BF)

        @pl.loop(0, L // 2, unroll=True)
        def _(zz):
            two = pl.ds(2 * zz, 2)
            plane = phi[0, two].astype(F32) * weights[0]
            for i in range(1, B):
                plane = plane + phi[i, two].astype(F32) * weights[i]
            flat[pl.ds(pl.multiple_of(2 * N * zz, 2 * N), 2 * N)] = (
                plane[:, :, :128].reshape(2 * N, 128).astype(BF)
            )
            tail = [
                jnp.concatenate([plane[b, 40 * q : 40 * q + 40, 128:] for q in range(4)], axis=1)
                for b in range(2)
            ]
            flat[pl.ds(pl.multiple_of(N * L + 80 * zz, 80), 80)] = (
                jnp.concatenate(tail, axis=0).astype(BF)
            )

    def unpack(j):
        @pl.loop(0, L // 2, unroll=True)
        def _(zz):
            main = gathered[j, pl.ds(pl.multiple_of(2 * N * zz, 2 * N), 2 * N)].astype(F32)
            par[j, pl.ds(2 * zz, 2), :, :128] = main.reshape(2, N, 128)
            tail = gathered[j, pl.ds(pl.multiple_of(N * L + 80 * zz, 80), 80)].astype(F32)
            for b in range(2):
                for q in range(4):
                    par[j, 2 * zz + b, 40 * q : 40 * q + 40, 128:] = tail[
                        40 * b : 40 * b + 40, 32 * q : 32 * q + 32
                    ]

    def coulomb():
        scale = (2.0 * math.pi / (N * spacing)) ** 2
        size = 4.0 * math.pi / (scale * N**3)
        z = lax.broadcasted_iota(jnp.int32, (N, 256), 0)
        lane = lax.broadcasted_iota(jnp.int32, (N, 256), 1)
        z = jnp.minimum(z, N - z)
        second = lane >> 7
        lane = lane & 127

        @pl.loop(0, L // 2, unroll=True)
        def _(kp):
            x = ((2 * kp + second) * S + me + 1) >> 1
            for u, y in enumerate(((lane + LOW + 1) >> 1, ((lane & (LOW - 1)) + 1) >> 1)):
                g = (z * z + x * x + y * y).astype(F32)
                kern[u, kp] = jnp.where(g > 0, size / jnp.where(g > 0, g, 1.0), 0.0)

    def place(row):
        return lax.div(row, 8), pl.ds(lax.rem(row, 8), N, stride=8)

    def turn_tables():
        for h in range(2):
            for i in range(B):
                tyi[h, i] = tyf[h, i].astype(F32).T.astype(BF)
                tzi[h, i] = tzf[i, N * h : N * (h + 1)].astype(F32).T.astype(BF)
                tli[h, i] = tlf[i, N * h : N * (h + 1)].astype(F32).T.astype(BF)

    def flush(j, t):
        @pl.loop(0, S)
        def _(d):
            block = stage[t, pl.ds(d * 8 * L, 8 * L)].reshape(L, 8, 128)
            send[j, t, pl.ds(d * L, L)] = block.astype(BF)

        recv[j, t, me] = send[j, t, pl.ds(me * L, L)]

        @pl.loop(1, S)
        def _(k):
            d = lax.rem(me + k, S)
            remote(send.at[j, t, pl.ds(d * L, L)], recv.at[j, t, me], j, t, d).start()

    def each_extra(d, move):
        base = d * 8 * L
        for o in range(2):
            for b in range(2):
                move((d, o, slice(4 * b, 4 * b + 4)), (6, pl.ds(base + 8 * o + b, 4, stride=16)))
                move((d, 2 + o, pl.ds(4 * b, 1)), (6, pl.ds(base + 64 + 8 * o + b, 1)))
                move((d, 2 + o, pl.ds(4 * b + 1, 1)), (6, pl.ds(base + 8 * o + 2 + b, 1)))
        move((d, 4), (7, pl.ds(base, 8)))

    def flush_extra(j):
        @pl.loop(0, S)
        def _(d):
            def move(to, source):
                extra[to] = stage[source]

            each_extra(d, move)
            send_x[j, d] = extra[d].astype(BF)

        recv_x[j, me] = send_x[j, me]

        @pl.loop(1, S)
        def _(k):
            d = lax.rem(me + k, S)
            remote(send_x.at[j, d], recv_x.at[j, me], j, TILES, d).start()

    def residual_row(zz):
        return 2 * zz + jnp.where(zz < 4, 56, 42)

    def forward(j, between):
        rest[...] = jnp.zeros((L, N, 128), F32)

        @pl.loop(0, B)
        def _(i):
            @pl.loop(0, L // 2, unroll=True)
            def _(zz):
                two = pl.ds(2 * zz, 2)
                density = phi[i, two].astype(F32) * par[j, two]
                high, low = halves(density.reshape(2 * N, N))
                y = dot(high, tyf[0, i]) + dot(low, tyf[0, i]) + dot(high, tyf[1, i])
                rest[two] += y[:, 128:].reshape(2, N, 128)
                main = jnp.concatenate([y[:N, :128], y[N:, :128]], axis=1)
                x = left(txf[...], main)
                for b in range(2):
                    t, at = place(i * L + 2 * zz + b)
                    stage[t, at, :] = x[:, 128 * b : 128 * (b + 1)]

            flush(j, i)
            for n, step in enumerate(between):
                pl.when(i == n + 1)(step)

        flush(j, B)

        @pl.loop(0, L // 2, unroll=True)
        def _(zz):
            low = jnp.concatenate([rest[2 * zz], rest[2 * zz + 1]], axis=1)
            x = left(txf[...], low)
            left_over = x - x.astype(BF).astype(F32)
            for b in range(2):
                t, at = place(B * L + 2 * zz + b)
                stage[t, at, :] = x[:, 128 * b : 128 * (b + 1)]
                t, at = place(residual_row(zz) + b)
                stage[t, at, :] = left_over[:, 128 * b : 128 * (b + 1)]

        flush(j, B + 1)
        flush_extra(j)

    def arrived(j, t):
        others = recv.at[j, t, pl.ds(0, S - 1)]
        remote(others, others, j, t, 0).wait_recv()

    def returned(j, t):
        others = recv.at[j, t, pl.ds(0, S - 1)]
        remote(others, others, 2 + j, t, 0).wait_recv()

    others_x = recv_x.at[0, pl.ds(0, S - 1)]

    def middle(j):
        def load(pieces):
            return jnp.concatenate(
                [
                    jnp.concatenate(
                        [piece(b).astype(F32).reshape(128, 128) for piece in pieces], axis=0
                    )
                    for b in range(2)
                ],
                axis=1,
            ).astype(BF)

        def tile(kp, t):
            return lambda b: recv[j, t, :, 2 * kp + b]

        def extra_tile(t):
            return lambda b: recv_x[j, :, t + b]

        def residual_tile(b):
            if b:
                return jnp.zeros((S, 8, 128), BF)
            return recv_x[j, :, 4]

        def parts(value):
            for b in range(2):
                yield b, value[:, 128 * b : 128 * (b + 1)].reshape(S, 8, 128).astype(BF)

        def leave(kp, t, value):
            for b, part in parts(value):
                back[j, t, :, 2 * kp + b] = part

        def leave_extra(t, value):
            for b, part in parts(value):
                back_x[j, :, t + b] = part

        def ship(t):
            home[j, t, pl.ds(me * L, L)] = back[j, t, me]

            @pl.loop(1, S)
            def _(k):
                d = lax.rem(me + k, S)
                remote(back.at[j, t, d], home.at[j, t, pl.ds(me * L, L)], 2 + j, t, d).start()

        def apply(table, spectrum):
            high, low = halves(spectrum)
            return dot(table(0), high) + dot(table(1), high) + dot(table(0), low)

        def low_modes(kp, v, t, residual):
            spectrum = fold(dot(tlf[v], load((tile(kp, B + 1), extra_tile(t)))))
            if residual:
                spectrum += fold(dot(tlf[1], load((residual_tile, extra_tile(2)))))
            spectrum *= kern[1, kp]
            w = apply(lambda h: tli[h, v], spectrum)
            leave(kp, B + 1, w[:128])
            if residual:
                r = apply(lambda h: tli[h, 1], spectrum)
                r -= r.astype(BF).astype(F32)
                back_x[j, :, 4] = r[:128, :128].reshape(S, 8, 128).astype(BF)
                extra_sum[1] = r[128:]
            return w[128:]

        arrived(j, B + 1)
        remote(others_x, others_x, j, TILES, 0).wait_recv()
        extra_sum[0] = low_modes(0, 0, 0, True)

        @pl.loop(1, 4)
        def _(kp):
            extra_sum[0] += low_modes(kp, kp, 0, False)

        extra_sum[1] += low_modes(4, 0, 2, False)
        for n in range(2):
            leave_extra(2 * n, extra_sum[n])
        ship(B + 1)
        home_x[j, me] = back_x[j, me]

        @pl.loop(1, S)
        def _(k):
            d = lax.rem(me + k, S)
            remote(back_x.at[j, d], home_x.at[j, me], 2 + j, TILES, d).start()

        arrived(j, 0)
        carry[...] = jnp.zeros((L // 2, 128, 256), F32)

        @pl.loop(0, B)
        def _(i):
            arrived(j, i + 1)

            @pl.loop(0, L // 2, unroll=True)
            def _(kp):
                spectrum = fold(dot(tzf[i], load((tile(kp, i), tile(kp, i + 1)))))
                w = apply(lambda h: tzi[h, i], spectrum * kern[0, kp])
                leave(kp, i, carry[kp] + w[:128])
                carry[kp] = w[128:]

            ship(i)

        @pl.loop(0, L // 2, unroll=True)
        def _(kp):
            leave(kp, B, carry[kp])

        ship(B)

    def inverse(j):
        def unstage(t):
            @pl.loop(0, S)
            def _(c):
                block = home[j, t, pl.ds(c * L, L)].astype(F32)
                stage[t, pl.ds(c * 8 * L, 8 * L)] = block.reshape(8 * L, 128)

        def planes(row):
            got = []
            for b in range(2):
                t, at = place(row + b)
                got.append(stage[t, at, :])
            return jnp.concatenate(got, axis=1).astype(BF)

        returned(j, B + 1)
        unstage(B + 1)
        for t in (6, 7):
            stage[t] = jnp.zeros((8 * N, 128), F32)
        remote(others_x, others_x, 2 + j, TILES, 0).wait_recv()

        @pl.loop(0, S)
        def _(d):
            extra[d] = home_x[j, d].astype(F32)

            def move(source, to):
                stage[to] = extra[source]

            each_extra(d, move)

        @pl.loop(0, L // 2, unroll=True)
        def _(zz):
            low_y = fold(dot(txi[...], planes(B * L + 2 * zz)))
            low_y += dot(txi[:N], planes(residual_row(zz)))
            for h, part in enumerate(halves(low_y)):
                for b in range(2):
                    rest_parts[h, 2 * zz + b] = part[:, 128 * b : 128 * (b + 1)]

        returned(j, 0)
        unstage(0)

        @pl.loop(0, B)
        def _(i):
            returned(j, i + 1)
            unstage(i + 1)

            @pl.loop(0, L // 2, unroll=True)
            def _(zz):
                two = pl.ds(2 * zz, 2)
                main = halves(fold(dot(txi[...], planes(i * L + 2 * zz))))
                high, low = (
                    jnp.concatenate(
                        [
                            jnp.concatenate(
                                [main[h][:, 128 * b : 128 * (b + 1)], rest_parts[h, 2 * zz + b]],
                                axis=1,
                            )
                            for b in range(2)
                        ],
                        axis=0,
                    )
                    for h in range(2)
                )
                v = dot(high, tyi[0, i]) + dot(low, tyi[0, i]) + dot(high, tyi[1, i])
                v = v.reshape(2, N, N) * par[j, two]
                if j == 0:
                    total[i, two] = v
                else:
                    out[i, two] = (-0.25 * (total[i, two] + v)).astype(BF)

            if j == 1:
                pltpu.make_async_copy(out.at[i], result.at[i], out_sem.at[i]).start()

    first = owner[0] == last
    index_a = jnp.where(first, index[0], index[1])
    index_b = jnp.where(first, index[1], index[0])
    owner_b = jnp.where(first, owner[1], owner[0])
    others = gathered.at[0, pl.ds(0, (bands - 1) * CH)]
    ring = bands // 2
    wide = 2 * CH
    most = gathered.at[1, pl.ds(0, (ring - 1) * wide)]
    along = lax.rem(band, ring)
    start = band - along
    loads[0].wait()

    @pl.when(band == last)
    def _():
        pick(chosen, [jnp.where(index_a == i, 1.0, 0.0) for i in range(B)])

    pl.semaphore_wait(barrier, S + bands - 2)

    @pl.when(band == last)
    def _():
        @pl.loop(1, bands)
        def _(k):
            c = lax.rem(band + k, bands)
            share(chosen.at[chunk(c)], gathered.at[0, chunk(c)], 0, c).start()

        gathered[0, chunk(last)] = chosen[chunk(last)]

    is_b = owner_b == band
    pick(masked, [jnp.where((index_b == i) & is_b, 1.0, 0.0) for i in range(B)])

    @pl.when(band != last)
    def _():
        mine = gathered.at[0, chunk(band)]
        share(mine, mine, 0, 0).wait_recv()

    @pl.loop(1, bands)
    def _(k):
        mine = gathered.at[0, chunk(band)]
        share(mine, mine, 1, lax.rem(band + k, bands)).start()

    @pl.loop(1, ring)
    def _(k):
        c = lax.rem(along + k, ring)
        share(masked.at[block(c)], heap.at[along], 2, start + c).start()

    coulomb()
    for load in loads[1:]:
        load.wait()
    turn_tables()
    share(others, others, 1, 0).wait_recv()

    unpack(0)

    def reduce_b():
        share(most, most, 2, 0).wait_recv()
        heap[along] = masked[block(along)]
        whole = heap[0].astype(F32)
        for s in range(1, ring):
            whole = whole + heap[s].astype(F32)
        part_b[...] = whole.astype(BF)
        share(part_b, other_b, 3, lax.rem(band + ring, bands)).start()

    def gather_b():
        share(part_b, other_b, 3, 0).wait_recv()
        whole = part_b[...].astype(F32) + other_b[...].astype(F32)
        mine = gathered.at[1, block(along)]
        mine[...] = whole.astype(BF)

        @pl.loop(1, ring)
        def _(k):
            share(mine, mine, 4, start + lax.rem(along + k, ring)).start()

    extra[...] = jnp.zeros((S, EXTRA, 8, 128), F32)
    forward(0, (reduce_b, gather_b))
    share(most, most, 4, 0).wait_recv()
    unpack(1)
    forward(1, ())
    for j in range(2):
        middle(j)
    for j in range(2):
        inverse(j)
    for j in range(2):
        for t in range(TILES):
            sent = recv.at[j, t, pl.ds(0, S - 1)]
            remote(sent, sent, j, t, 0).wait_send()
            remote(sent, sent, 2 + j, t, 0).wait_send()
        remote(others_x, others_x, j, TILES, 0).wait_send()
        remote(others_x, others_x, 2 + j, TILES, 0).wait_send()
    for i in range(B):
        pltpu.make_async_copy(out.at[i], result.at[i], out_sem.at[i]).wait()
    share(others, others, 1, 0).wait_send()
    share(most, most, 2, 0).wait_send()
    share(part_b, part_b, 3, 0).wait_send()
    share(most, most, 4, 0).wait_send()

    @pl.when(band == last)
    def _():
        share(others, others, 0, 0).wait_send()


def solve(orbitals, owner, index):
    tables = [jnp.asarray(t) for t in make_tables()]
    smem = pl.BlockSpec(memory_space=pltpu.SMEM)
    hbm = pl.BlockSpec(memory_space=pl.ANY)
    bands = lax.axis_size("band")
    return pl.pallas_call(
        solve_kernel,
        out_shape=jax.ShapeDtypeStruct(orbitals.shape, BF),
        in_specs=[smem, smem] + [hbm] * (1 + len(tables)),
        out_specs=hbm,
        scratch_shapes=[pltpu.VMEM(orbitals.shape, BF)] * 2
        + [pltpu.VMEM(t.shape, BF) for t in tables]
        + [
            pltpu.VMEM((2, B, 256, N), BF),
            pltpu.VMEM((2, B, 256, N), BF),
            pltpu.VMEM((2, 4, 256, N), BF),
            pltpu.VMEM((bands * CH, 128), BF),
            pltpu.VMEM((bands * CH, 128), BF),
            pltpu.VMEM((bands // 2, 2 * CH, 128), BF),
            pltpu.VMEM((2 * CH, 128), BF),
            pltpu.VMEM((2 * CH, 128), BF),
            pltpu.VMEM((2, bands * CH, 128), BF),
            pltpu.VMEM((2, L, N, N), F32),
            pltpu.VMEM((2, TILES, N, 8, 128), BF),
            pltpu.VMEM((2, TILES, S, L, 8, 128), BF),
            pltpu.VMEM((2, TILES, S, L, 8, 128), BF),
            pltpu.VMEM((2, TILES, N, 8, 128), BF),
            pltpu.VMEM((2, S, EXTRA, 8, 128), BF),
            pltpu.VMEM((2, S, EXTRA, 8, 128), BF),
            pltpu.VMEM((2, S, EXTRA, 8, 128), BF),
            pltpu.VMEM((2, S, EXTRA, 8, 128), BF),
            pltpu.VMEM((8, 8 * N, 128), F32),
            pltpu.VMEM((S, EXTRA, 8, 128), F32),
            pltpu.VMEM((2, 128, 256), F32),
            pltpu.VMEM((L, N, 128), F32),
            pltpu.VMEM((2, L, N, 128), BF),
            pltpu.VMEM((L // 2, 128, 256), F32),
            pltpu.VMEM((B, L, N, N), F32),
            pltpu.VMEM((2, L // 2, N, 256), F32),
            pltpu.SemaphoreType.DMA((1 + len(tables),)),
            pltpu.SemaphoreType.DMA((B,)),
            pltpu.SemaphoreType.DMA((4, TILES + 1)),
            pltpu.SemaphoreType.DMA((4, TILES + 1)),
            pltpu.SemaphoreType.DMA((5,)),
            pltpu.SemaphoreType.DMA((5,)),
        ],
        compiler_params=pltpu.CompilerParams(
            collective_id=0, has_side_effects=True, vmem_limit_bytes=60 << 20
        ),
        name="solve_pairs",
    )(owner, index, orbitals, *tables)


def per_device(orbitals, owner, index):
    return solve(orbitals, owner, index)


def solution(mesh):
    placed = (P("band", "slab", None, None), P(), P())
    return jax.shard_map(
        per_device,
        mesh=mesh,
        in_specs=placed,
        out_specs=P("band", "slab", None, None),
        check_vma=False,
    )
```

```python
import math

import jax
import jax.numpy as jnp
import ml_dtypes
import numpy as np
from jax import lax
from jax.experimental import pallas as pl
from jax.experimental.pallas import tpu as pltpu
from jax.sharding import PartitionSpec as P

spacing = 0.293125
MESH = pl.DeviceIdType.MESH
CH = 128
BF = jnp.bfloat16
F32 = jnp.float32
N = 160
S = 16
L = N // S
B = 4
LOW = 32
TILES = 6
EXTRA = 5


def split_table(table):
    high = table.astype(ml_dtypes.bfloat16)
    low = (table - high.astype(np.float64)).astype(ml_dtypes.bfloat16)
    return high, low


def make_tables():
    steps = np.arange(N)
    angle = 2.0 * np.pi / N * (steps[:, None] * steps[None, :] % N)
    cas = np.cos(angle) + np.sin(angle)
    by_size = np.array([(c + 1) // 2 if c % 2 else (N - c // 2) % N for c in range(N)])
    along_y = cas[by_size]
    ty = np.zeros((B, N, 256))
    for q in range(B):
        ty[q, :, :128] = along_y[LOW:].T
        ty[q, :, 128 + LOW * q : 128 + LOW * (q + 1)] = along_y[:LOW].T
    rows = np.array([by_size[(r % L) * S + r // L] for r in range(N)])
    tx = cas[rows]
    tz = np.zeros((B, N, 2, S, 8))
    for i in range(B):
        for h in range(2):
            for e in range(8):
                z = 8 * (i + h) + e - L * i
                if 0 <= z < L:
                    for s in range(S):
                        tz[i, :, h, s, e] = cas[:, s * L + z]
    tl = np.zeros((4, N, 2, S, 8))
    for v in range(4):
        for s in range(S):
            tl[v, :, 0, s] = cas[:, s * L : s * L + 8]
            tl[v, :, 1, s, v] = cas[:, s * L + 8]
            tl[v, :, 1, s, 4 + v] = cas[:, s * L + 9]
    tz = tz.reshape(B, N, 256)
    tl = tl.reshape(4, N, 256)
    stack = lambda t, axis: np.concatenate(split_table(t), axis=axis)
    pair = lambda t: np.stack(split_table(t))
    return pair(ty), stack(tx, 0), stack(tx.T, 0), stack(tz, 1), stack(tl, 1)


def both_ways(count):
    steps = []
    for k in range(count // 2, 0, -1):
        steps += [k, count - k] if 2 * k != count else [k]
    return steps


def dot(a, b):
    return jnp.dot(a, b, preferred_element_type=F32)


def halves(value):
    high = value.astype(BF)
    return high, (value - high.astype(F32)).astype(BF)


def fold(both):
    return both[:N] + both[N:]


def left(table, value):
    high, low = halves(value)
    return fold(dot(table, high)) + dot(table[:N], low)


def solve_kernel(
    owner, index, orbitals, *refs
):
    tables, result, phi, out = refs[:5], refs[5], refs[6], refs[7]
    tyf, txf, txi, tzf, tlf = held = refs[8:13]
    (
        tyi, tzi, tli, chosen, masked, heap, part_b, other_b, gathered, par,
        send, recv, back, home, send_x, recv_x, back_x, home_x,
        stage, extra, extra_sum, rest, rest_parts, carry, total, kern,
        load_sem, out_sem, send_sem, recv_sem, share_send, share_recv,
    ) = refs[13:]
    loads = [
        pltpu.make_async_copy(src, dst, load_sem.at[n])
        for n, (src, dst) in enumerate(zip((orbitals,) + tables, (phi,) + held))
    ]
    for load in loads:
        load.start()
    me = lax.axis_index("slab")
    band = lax.axis_index("band")
    bands = lax.axis_size("band")
    last = bands - 1
    barrier = pltpu.get_barrier_semaphore()

    @pl.loop(1, S)
    def _(k):
        pl.semaphore_signal(
            barrier, inc=1, device_id={"slab": lax.rem(me + k, S)}, device_id_type=MESH
        )

    @pl.loop(1, bands)
    def _(k):
        pl.semaphore_signal(
            barrier, inc=1, device_id={"band": lax.rem(band + k, bands)}, device_id_type=MESH
        )

    def remote(src, dst, which, t, d):
        return pltpu.make_async_remote_copy(
            src_ref=src,
            dst_ref=dst,
            send_sem=send_sem.at[which, t],
            recv_sem=recv_sem.at[which, t],
            device_id={"slab": d},
            device_id_type=MESH,
        )

    def share(src, dst, which, d):
        return pltpu.make_async_remote_copy(
            src_ref=src,
            dst_ref=dst,
            send_sem=share_send.at[which],
            recv_sem=share_recv.at[which],
            device_id={"band": d},
            device_id_type=MESH,
        )

    def chunk(c):
        return pl.ds(pl.multiple_of(c * CH, CH), CH)

    def block(c):
        return pl.ds(pl.multiple_of(c * 2 * CH, 2 * CH), 2 * CH)

    def pick(flat, weights):
        flat[pl.ds(N * L * 5 // 4, 48)] = jnp.zeros((48, 128), BF)

        @pl.loop(0, L // 2, unroll=True)
        def _(zz):
            two = pl.ds(2 * zz, 2)
            plane = phi[0, two].astype(F32) * weights[0]
            for i in range(1, B):
                plane = plane + phi[i, two].astype(F32) * weights[i]
            flat[pl.ds(pl.multiple_of(2 * N * zz, 2 * N), 2 * N)] = (
                plane[:, :, :128].reshape(2 * N, 128).astype(BF)
            )
            tail = [
                jnp.concatenate([plane[b, 40 * q : 40 * q + 40, 128:] for q in range(4)], axis=1)
                for b in range(2)
            ]
            flat[pl.ds(pl.multiple_of(N * L + 80 * zz, 80), 80)] = (
                jnp.concatenate(tail, axis=0).astype(BF)
            )

    def unpack(j):
        @pl.loop(0, L // 2, unroll=True)
        def _(zz):
            main = gathered[j, pl.ds(pl.multiple_of(2 * N * zz, 2 * N), 2 * N)].astype(F32)
            par[j, pl.ds(2 * zz, 2), :, :128] = main.reshape(2, N, 128)
            tail = gathered[j, pl.ds(pl.multiple_of(N * L + 80 * zz, 80), 80)].astype(F32)
            for b in range(2):
                for q in range(4):
                    par[j, 2 * zz + b, 40 * q : 40 * q + 40, 128:] = tail[
                        40 * b : 40 * b + 40, 32 * q : 32 * q + 32
                    ]

    def coulomb():
        scale = (2.0 * math.pi / (N * spacing)) ** 2
        size = 4.0 * math.pi / (scale * N**3)
        z = lax.broadcasted_iota(jnp.int32, (N, 256), 0)
        lane = lax.broadcasted_iota(jnp.int32, (N, 256), 1)
        z = jnp.minimum(z, N - z)
        second = lane >> 7
        lane = lane & 127

        @pl.loop(0, L // 2, unroll=True)
        def _(kp):
            x = ((2 * kp + second) * S + me + 1) >> 1
            for u, y in enumerate(((lane + LOW + 1) >> 1, ((lane & (LOW - 1)) + 1) >> 1)):
                g = (z * z + x * x + y * y).astype(F32)
                kern[u, kp] = jnp.where(g > 0, size / jnp.where(g > 0, g, 1.0), 0.0)

    def place(row):
        return lax.div(row, 8), pl.ds(lax.rem(row, 8), N, stride=8)

    def turn_tables():
        for h in range(2):
            for i in range(B):
                tyi[h, i] = tyf[h, i].astype(F32).T.astype(BF)
                tzi[h, i] = tzf[i, N * h : N * (h + 1)].astype(F32).T.astype(BF)
                tli[h, i] = tlf[i, N * h : N * (h + 1)].astype(F32).T.astype(BF)

    def flush(j, t):
        @pl.loop(0, S)
        def _(d):
            block = stage[t, pl.ds(d * 8 * L, 8 * L)].reshape(L, 8, 128)
            send[j, t, pl.ds(d * L, L)] = block.astype(BF)

        recv[j, t, me] = send[j, t, pl.ds(me * L, L)]

        @pl.loop(1, S)
        def _(k):
            d = lax.rem(me + k, S)
            remote(send.at[j, t, pl.ds(d * L, L)], recv.at[j, t, me], j, t, d).start()

    def each_extra(d, move):
        base = d * 8 * L
        for o in range(2):
            for b in range(2):
                move((d, o, slice(4 * b, 4 * b + 4)), (6, pl.ds(base + 8 * o + b, 4, stride=16)))
                move((d, 2 + o, pl.ds(4 * b, 1)), (6, pl.ds(base + 64 + 8 * o + b, 1)))
                move((d, 2 + o, pl.ds(4 * b + 1, 1)), (6, pl.ds(base + 8 * o + 2 + b, 1)))
        move((d, 4), (7, pl.ds(base, 8)))

    def flush_extra(j):
        @pl.loop(0, S)
        def _(d):
            def move(to, source):
                extra[to] = stage[source]

            each_extra(d, move)
            send_x[j, d] = extra[d].astype(BF)

        recv_x[j, me] = send_x[j, me]

        @pl.loop(1, S)
        def _(k):
            d = lax.rem(me + k, S)
            remote(send_x.at[j, d], recv_x.at[j, me], j, TILES, d).start()

    def residual_row(zz):
        return 2 * zz + jnp.where(zz < 4, 56, 42)

    def forward(j, between):
        rest[...] = jnp.zeros((L, N, 128), F32)

        @pl.loop(0, B)
        def _(i):
            @pl.loop(0, L // 2, unroll=True)
            def _(zz):
                two = pl.ds(2 * zz, 2)
                density = phi[i, two].astype(F32) * par[j, two]
                high, low = halves(density.reshape(2 * N, N))
                y = dot(high, tyf[0, i]) + dot(low, tyf[0, i]) + dot(high, tyf[1, i])
                rest[two] += y[:, 128:].reshape(2, N, 128)
                main = jnp.concatenate([y[:N, :128], y[N:, :128]], axis=1)
                x = left(txf[...], main)
                for b in range(2):
                    t, at = place(i * L + 2 * zz + b)
                    stage[t, at, :] = x[:, 128 * b : 128 * (b + 1)]

            flush(j, i)
            for n, step in enumerate(between):
                pl.when(i == n + 1)(step)

        flush(j, B)

        @pl.loop(0, L // 2, unroll=True)
        def _(zz):
            low = jnp.concatenate([rest[2 * zz], rest[2 * zz + 1]], axis=1)
            x = left(txf[...], low)
            left_over = x - x.astype(BF).astype(F32)
            for b in range(2):
                t, at = place(B * L + 2 * zz + b)
                stage[t, at, :] = x[:, 128 * b : 128 * (b + 1)]
                t, at = place(residual_row(zz) + b)
                stage[t, at, :] = left_over[:, 128 * b : 128 * (b + 1)]

        flush(j, B + 1)
        flush_extra(j)

    def arrived(j, t):
        others = recv.at[j, t, pl.ds(0, S - 1)]
        remote(others, others, j, t, 0).wait_recv()

    def returned(j, t):
        others = recv.at[j, t, pl.ds(0, S - 1)]
        remote(others, others, 2 + j, t, 0).wait_recv()

    others_x = recv_x.at[0, pl.ds(0, S - 1)]

    def middle(j):
        def load(pieces):
            return jnp.concatenate(
                [
                    jnp.concatenate(
                        [piece(b).astype(F32).reshape(128, 128) for piece in pieces], axis=0
                    )
                    for b in range(2)
                ],
                axis=1,
            ).astype(BF)

        def tile(kp, t):
            return lambda b: recv[j, t, :, 2 * kp + b]

        def extra_tile(t):
            return lambda b: recv_x[j, :, t + b]

        def residual_tile(b):
            if b:
                return jnp.zeros((S, 8, 128), BF)
            return recv_x[j, :, 4]

        def parts(value):
            for b in range(2):
                yield b, value[:, 128 * b : 128 * (b + 1)].reshape(S, 8, 128).astype(BF)

        def leave(kp, t, value):
            for b, part in parts(value):
                back[j, t, :, 2 * kp + b] = part

        def leave_extra(t, value):
            for b, part in parts(value):
                back_x[j, :, t + b] = part

        def ship(t):
            home[j, t, pl.ds(me * L, L)] = back[j, t, me]

            @pl.loop(1, S)
            def _(k):
                d = lax.rem(me + k, S)
                remote(back.at[j, t, d], home.at[j, t, pl.ds(me * L, L)], 2 + j, t, d).start()

        def apply(table, spectrum):
            high, low = halves(spectrum)
            return dot(table(0), high) + dot(table(1), high) + dot(table(0), low)

        def low_modes(kp, v, t, residual):
            spectrum = fold(dot(tlf[v], load((tile(kp, B + 1), extra_tile(t)))))
            if residual:
                spectrum += fold(dot(tlf[1], load((residual_tile, extra_tile(2)))))
            spectrum *= kern[1, kp]
            w = apply(lambda h: tli[h, v], spectrum)
            leave(kp, B + 1, w[:128])
            if residual:
                r = apply(lambda h: tli[h, 1], spectrum)
                r -= r.astype(BF).astype(F32)
                back_x[j, :, 4] = r[:128, :128].reshape(S, 8, 128).astype(BF)
                extra_sum[1] = r[128:]
            return w[128:]

        arrived(j, B + 1)
        remote(others_x, others_x, j, TILES, 0).wait_recv()
        extra_sum[0] = low_modes(0, 0, 0, True)

        @pl.loop(1, 4)
        def _(kp):
            extra_sum[0] += low_modes(kp, kp, 0, False)

        extra_sum[1] += low_modes(4, 0, 2, False)
        for n in range(2):
            leave_extra(2 * n, extra_sum[n])
        ship(B + 1)
        home_x[j, me] = back_x[j, me]

        @pl.loop(1, S)
        def _(k):
            d = lax.rem(me + k, S)
            remote(back_x.at[j, d], home_x.at[j, me], 2 + j, TILES, d).start()

        arrived(j, 0)
        carry[...] = jnp.zeros((L // 2, 128, 256), F32)

        @pl.loop(0, B)
        def _(i):
            arrived(j, i + 1)

            @pl.loop(0, L // 2, unroll=True)
            def _(kp):
                spectrum = fold(dot(tzf[i], load((tile(kp, i), tile(kp, i + 1)))))
                w = apply(lambda h: tzi[h, i], spectrum * kern[0, kp])
                leave(kp, i, carry[kp] + w[:128])
                carry[kp] = w[128:]

            ship(i)

        @pl.loop(0, L // 2, unroll=True)
        def _(kp):
            leave(kp, B, carry[kp])

        ship(B)

    def inverse(j):
        def unstage(t):
            @pl.loop(0, S)
            def _(c):
                block = home[j, t, pl.ds(c * L, L)].astype(F32)
                stage[t, pl.ds(c * 8 * L, 8 * L)] = block.reshape(8 * L, 128)

        def planes(row):
            got = []
            for b in range(2):
                t, at = place(row + b)
                got.append(stage[t, at, :])
            return jnp.concatenate(got, axis=1).astype(BF)

        returned(j, B + 1)
        unstage(B + 1)
        for t in (6, 7):
            stage[t] = jnp.zeros((8 * N, 128), F32)
        remote(others_x, others_x, 2 + j, TILES, 0).wait_recv()

        @pl.loop(0, S)
        def _(d):
            extra[d] = home_x[j, d].astype(F32)

            def move(source, to):
                stage[to] = extra[source]

            each_extra(d, move)

        @pl.loop(0, L // 2, unroll=True)
        def _(zz):
            low_y = fold(dot(txi[...], planes(B * L + 2 * zz)))
            low_y += dot(txi[:N], planes(residual_row(zz)))
            for h, part in enumerate(halves(low_y)):
                for b in range(2):
                    rest_parts[h, 2 * zz + b] = part[:, 128 * b : 128 * (b + 1)]

        returned(j, 0)
        unstage(0)

        @pl.loop(0, B)
        def _(i):
            returned(j, i + 1)
            unstage(i + 1)

            @pl.loop(0, L // 2, unroll=True)
            def _(zz):
                two = pl.ds(2 * zz, 2)
                main = halves(fold(dot(txi[...], planes(i * L + 2 * zz))))
                high, low = (
                    jnp.concatenate(
                        [
                            jnp.concatenate(
                                [main[h][:, 128 * b : 128 * (b + 1)], rest_parts[h, 2 * zz + b]],
                                axis=1,
                            )
                            for b in range(2)
                        ],
                        axis=0,
                    )
                    for h in range(2)
                )
                v = dot(high, tyi[0, i]) + dot(low, tyi[0, i]) + dot(high, tyi[1, i])
                v = v.reshape(2, N, N) * par[j, two]
                if j == 0:
                    total[i, two] = v
                else:
                    out[i, two] = (-0.25 * (total[i, two] + v)).astype(BF)

            if j == 1:
                pltpu.make_async_copy(out.at[i], result.at[i], out_sem.at[i]).start()

    first = owner[0] == last
    index_a = jnp.where(first, index[0], index[1])
    index_b = jnp.where(first, index[1], index[0])
    owner_b = jnp.where(first, owner[1], owner[0])
    others = gathered.at[0, pl.ds(0, (bands - 1) * CH)]
    ring = bands // 2
    wide = 2 * CH
    most = gathered.at[1, pl.ds(0, (ring - 1) * wide)]
    along = lax.rem(band, ring)
    start = band - along
    loads[0].wait()

    @pl.when(band == last)
    def _():
        pick(chosen, [jnp.where(index_a == i, 1.0, 0.0) for i in range(B)])

    pl.semaphore_wait(barrier, S + bands - 2)

    @pl.when(band == last)
    def _():
        @pl.loop(1, bands)
        def _(k):
            c = lax.rem(band + k, bands)
            share(chosen.at[chunk(c)], gathered.at[0, chunk(c)], 0, c).start()

        gathered[0, chunk(last)] = chosen[chunk(last)]

    is_b = owner_b == band
    pick(masked, [jnp.where((index_b == i) & is_b, 1.0, 0.0) for i in range(B)])

    coulomb()
    for load in loads[1:]:
        load.wait()

    @pl.when(band != last)
    def _():
        mine = gathered.at[0, chunk(band)]
        share(mine, mine, 0, 0).wait_recv()

    mine_a = gathered.at[0, chunk(band)]
    for k in both_ways(bands):
        share(mine_a, mine_a, 1, lax.rem(band + k, bands)).start()

    for k in both_ways(ring):
        c = lax.rem(along + k, ring)
        share(masked.at[block(c)], heap.at[along], 2, start + c).start()

    turn_tables()
    extra[...] = jnp.zeros((S, EXTRA, 8, 128), F32)
    share(others, others, 1, 0).wait_recv()

    unpack(0)

    def reduce_b():
        share(most, most, 2, 0).wait_recv()
        heap[along] = masked[block(along)]
        whole = heap[0].astype(F32)
        for s in range(1, ring):
            whole = whole + heap[s].astype(F32)
        part_b[...] = whole.astype(BF)
        share(part_b, other_b, 3, lax.rem(band + ring, bands)).start()

    def gather_b():
        share(part_b, other_b, 3, 0).wait_recv()
        whole = part_b[...].astype(F32) + other_b[...].astype(F32)
        mine = gathered.at[1, block(along)]
        mine[...] = whole.astype(BF)

        for k in both_ways(ring):
            share(mine, mine, 4, start + lax.rem(along + k, ring)).start()

    forward(0, (reduce_b, gather_b))
    share(most, most, 4, 0).wait_recv()
    unpack(1)
    forward(1, ())
    for j in range(2):
        middle(j)
    for j in range(2):
        inverse(j)
    for j in range(2):
        for t in range(TILES):
            sent = recv.at[j, t, pl.ds(0, S - 1)]
            remote(sent, sent, j, t, 0).wait_send()
            remote(sent, sent, 2 + j, t, 0).wait_send()
        remote(others_x, others_x, j, TILES, 0).wait_send()
        remote(others_x, others_x, 2 + j, TILES, 0).wait_send()
    for i in range(B):
        pltpu.make_async_copy(out.at[i], result.at[i], out_sem.at[i]).wait()
    share(others, others, 1, 0).wait_send()
    share(most, most, 2, 0).wait_send()
    share(part_b, part_b, 3, 0).wait_send()
    share(most, most, 4, 0).wait_send()

    @pl.when(band == last)
    def _():
        share(others, others, 0, 0).wait_send()


def solve(orbitals, owner, index):
    tables = [jnp.asarray(t) for t in make_tables()]
    smem = pl.BlockSpec(memory_space=pltpu.SMEM)
    hbm = pl.BlockSpec(memory_space=pl.ANY)
    bands = lax.axis_size("band")
    return pl.pallas_call(
        solve_kernel,
        out_shape=jax.ShapeDtypeStruct(orbitals.shape, BF),
        in_specs=[smem, smem] + [hbm] * (1 + len(tables)),
        out_specs=hbm,
        scratch_shapes=[pltpu.VMEM(orbitals.shape, BF)] * 2
        + [pltpu.VMEM(t.shape, BF) for t in tables]
        + [
            pltpu.VMEM((2, B, 256, N), BF),
            pltpu.VMEM((2, B, 256, N), BF),
            pltpu.VMEM((2, 4, 256, N), BF),
            pltpu.VMEM((bands * CH, 128), BF),
            pltpu.VMEM((bands * CH, 128), BF),
            pltpu.VMEM((bands // 2, 2 * CH, 128), BF),
            pltpu.VMEM((2 * CH, 128), BF),
            pltpu.VMEM((2 * CH, 128), BF),
            pltpu.VMEM((2, bands * CH, 128), BF),
            pltpu.VMEM((2, L, N, N), F32),
            pltpu.VMEM((2, TILES, N, 8, 128), BF),
            pltpu.VMEM((2, TILES, S, L, 8, 128), BF),
            pltpu.VMEM((2, TILES, S, L, 8, 128), BF),
            pltpu.VMEM((2, TILES, N, 8, 128), BF),
            pltpu.VMEM((2, S, EXTRA, 8, 128), BF),
            pltpu.VMEM((2, S, EXTRA, 8, 128), BF),
            pltpu.VMEM((2, S, EXTRA, 8, 128), BF),
            pltpu.VMEM((2, S, EXTRA, 8, 128), BF),
            pltpu.VMEM((8, 8 * N, 128), F32),
            pltpu.VMEM((S, EXTRA, 8, 128), F32),
            pltpu.VMEM((2, 128, 256), F32),
            pltpu.VMEM((L, N, 128), F32),
            pltpu.VMEM((2, L, N, 128), BF),
            pltpu.VMEM((L // 2, 128, 256), F32),
            pltpu.VMEM((B, L, N, N), F32),
            pltpu.VMEM((2, L // 2, N, 256), F32),
            pltpu.SemaphoreType.DMA((1 + len(tables),)),
            pltpu.SemaphoreType.DMA((B,)),
            pltpu.SemaphoreType.DMA((4, TILES + 1)),
            pltpu.SemaphoreType.DMA((4, TILES + 1)),
            pltpu.SemaphoreType.DMA((5,)),
            pltpu.SemaphoreType.DMA((5,)),
        ],
        compiler_params=pltpu.CompilerParams(
            collective_id=0, has_side_effects=True, vmem_limit_bytes=60 << 20
        ),
        name="solve_pairs",
    )(owner, index, orbitals, *tables)


def per_device(orbitals, owner, index):
    return solve(orbitals, owner, index)


def solution(mesh):
    placed = (P("band", "slab", None, None), P(), P())
    return jax.shard_map(
        per_device,
        mesh=mesh,
        in_specs=placed,
        out_specs=P("band", "slab", None, None),
        check_vma=False,
    )
```
